128 devices in a mesh: seq: 4 (over x), dec: 32 (over y, z, core).
Axes of the slice: x: 4, y: 4, z: 4, core: 2. Of those that a mesh axis runs over, the one named last changes fastest.
Arguments:
- latents: bfloat16 [4, 4, 3, 32, 1024], P('seq', None, None, 'dec'), may hold values from -6 to 6
- cache_lat: bfloat16 [4, 4, 3, 32, 512], P('seq', None, None, 'dec'), may hold values from -6 to 6
- cache_act: bfloat16 [4, 4, 3, 32, 12288], P('seq', None, None, 'dec'), may hold values from -0.25 to 2
- w_in: bfloat16 [27, 16, 384], replicated, may hold values from -0.3125 to 0.3125
- w_mid: bfloat16 [27, 384, 384], replicated, may hold values from -0.0625 to 0.0625
- norm_gain: float32 [384], replicated, may hold values from 0.1 to 1.9
- clip_group: int32 [4, 4], replicated, may hold values from 0 to 3, as said below
- band_rows: int32 [4, 32], replicated, may hold values from 2 to 24, as said below
Outputs:
- decoded: bfloat16 [4, 32, 24, 4, 16, 384], P('seq', 'dec')
The draws below stay inside these ranges and needn't reach their ends.
Inputs may be any that keep to these rules, and one draw needn't show every extreme that they name: For every sequence shard s, clip_group[s, :] names each of the 4 groups once. Each row of band_rows sums to 384; every band has 2 rows or more, and in each row one band has exactly 24 rows.
All inputs are finite; a program needn't handle non-finite values.
Results may differ from the reference program's by a relative error of at most 0.0029.
Values may be sent and summed in bfloat16 or wider, within the bound.
A program may use at most 192 MiB of HBM per device.

```python
import jax
import jax.numpy as jnp
from jax import lax

ZC = 16
C = 384
F = 4
CT = 2
COLS = 16
H = 96
RD = 3
STACK = 384
CLIPS = 16
BAND_MAX = 24
N_SEQ = 4
N_DEC = 32


def draw_clip_group(key, part):
    shard_keys = jax.vmap(lambda shard_index: jax.random.fold_in(key, shard_index))(jnp.arange(N_SEQ))
    return jax.vmap(lambda one_key: jax.random.permutation(one_key, N_SEQ))(shard_keys).astype(jnp.int32)


def band_counts(one_key):
    owners = N_DEC
    mean_rows = N_SEQ * H // N_DEC
    order_key, step_key = jax.random.split(one_key)
    owner_order = jax.random.permutation(order_key, owners)
    rank_ids = jnp.arange(owners - 1, dtype=jnp.int32)
    deduct = mean_rows * (rank_ids + 1) // (owners - 1) - mean_rows * rank_ids // (owners - 1)
    by_position = jnp.concatenate([jnp.full((1,), 2 * mean_rows, jnp.int32), (mean_rows - deduct).astype(jnp.int32)])
    pair_count = (owners - 1) // 2
    upper_rows = by_position[1:1 + 2 * pair_count:2]
    lower_rows = by_position[2:2 + 2 * pair_count:2]
    shifted = jax.random.randint(step_key, (pair_count,), 2 - upper_rows, lower_rows - 1, dtype=jnp.int32)
    by_position = by_position.at[1:1 + 2 * pair_count:2].add(shifted)
    by_position = by_position.at[2:2 + 2 * pair_count:2].add(-shifted)
    return jnp.zeros((owners,), jnp.int32).at[owner_order].set(by_position)


def draw_band_rows(key, part):
    group_keys = jax.vmap(lambda group_index: jax.random.fold_in(key, 1000 + group_index))(jnp.arange(N_SEQ))
    return jax.vmap(band_counts)(group_keys).astype(jnp.int32)


def block_levels(rng, extent, shards, smallest, largest):
    level, own = 1.0, jax.random.fold_in(rng, 6)
    for position, shards_of in shards:
        draws = jnp.exp(jax.random.uniform(jax.random.fold_in(own, position), (shards_of,), jnp.float32, smallest / len(shards), largest / len(shards)))
        level = level * jnp.repeat(draws, extent[position] // shards_of).reshape([-1 if axis == position else 1 for axis in range(len(extent))])
    return level


def centred(own_key, shape, scale, limit, cuts=(), held_as=jnp.bfloat16):
    entries = scale * jax.random.normal(own_key, shape, jnp.float32)
    if cuts:
        entries = entries * block_levels(own_key, shape, cuts, -0.22, 0.18)
    return jnp.clip(entries, -limit, limit).astype(held_as)


def setup_inputs(seed: int = 0) -> dict:
    streams_of = jax.random.split(jax.random.key(seed), 9)
    latents = centred(streams_of[0], (N_SEQ, N_SEQ, RD, N_DEC, F * COLS * ZC), 1.0, 6.0, ((0, 4), (3, 32)))
    cache_lat = centred(streams_of[1], (N_SEQ, N_SEQ, RD, N_DEC, CT * COLS * ZC), 1.0, 6.0, ((0, 4), (3, 32)))
    cache_act = jnp.clip(-0.25 + 2.25 * jax.random.uniform(streams_of[2], (N_SEQ, N_SEQ, RD, N_DEC, CT * COLS * C), jnp.float32) ** block_levels(streams_of[2], (N_SEQ, N_SEQ, RD, N_DEC, CT * COLS * C), ((0, 4), (3, 32)), -0.2, 0.2), -0.25, 2.0).astype(jnp.bfloat16)
    w_in = centred(streams_of[3], (27, ZC, C), (27 * ZC) ** -0.5, 0.3125)
    w_mid = centred(streams_of[4], (27, C, C), (27 * C) ** -0.5, 0.0625)
    norm_gain = jnp.clip(1.0 + 0.18 * jax.random.normal(streams_of[5], (C,), jnp.float32), 0.1, 1.9)
    clip_group = draw_clip_group(jax.random.fold_in(streams_of[8], 71), 0)
    band_rows = draw_band_rows(jax.random.fold_in(streams_of[8], 71), 0)
    return {"latents": latents, "cache_lat": cache_lat, "cache_act": cache_act, "w_in": w_in, "w_mid": w_mid, "norm_gain": norm_gain, "clip_group": clip_group, "band_rows": band_rows}


EPSILON = 1e-06

def causal_conv(frames_in, weights):
    row_count = frames_in.shape[0]
    padded = jnp.pad(frames_in, ((1, 1), (0, 0), (1, 1), (0, 0)))
    total_sum = jnp.zeros((row_count * F * COLS, weights.shape[2]), jnp.float32)
    for time_tap in range(3):
        for row_tap in range(3):
            for col_tap in range(3):
                tap_rows = padded[row_tap:row_tap + row_count, time_tap:time_tap + F, col_tap:col_tap + COLS, :]
                total_sum = total_sum + jnp.dot(tap_rows.reshape(row_count * F * COLS, weights.shape[1]), weights[time_tap * 9 + row_tap * 3 + col_tap], preferred_element_type=jnp.float32)
    return total_sum.reshape(row_count, F, COLS, weights.shape[2])

def decode_clip(inputs, w_in, w_mid, norm_gain):
    latent, old_lat, old_act = inputs
    layer_in = jnp.concatenate([old_lat.reshape(H, CT, COLS, ZC), latent.reshape(H, F, COLS, ZC)], axis=1)
    first_out = causal_conv(layer_in, w_in)
    mean_square = lax.optimization_barrier(jnp.mean(first_out * first_out, axis=-1, keepdims=True))
    activated = jax.nn.silu(first_out * lax.rsqrt(mean_square + EPSILON) * norm_gain).astype(jnp.bfloat16)
    conv_input = jnp.concatenate([old_act.reshape(H, CT, COLS, C), activated], axis=1)
    return (first_out + causal_conv(conv_input, w_mid)).astype(jnp.bfloat16)

def reference(latents, cache_lat, cache_act, w_in, w_mid, norm_gain, clip_group, band_rows):
    clip_lat = latents.reshape(CLIPS, H, F * COLS * ZC)
    clip_old = cache_lat.reshape(CLIPS, H, CT * COLS * ZC)
    clip_act = cache_act.reshape(CLIPS, H, CT * COLS * C)
    decoded_clips = lax.map(lambda inputs: decode_clip(inputs, w_in, w_mid, norm_gain), (clip_lat, clip_old, clip_act))
    decoded_clips = decoded_clips.reshape(N_SEQ, N_SEQ, H, F, COLS, C)
    group_ids = jnp.arange(N_SEQ, dtype=jnp.int32)
    match_group = clip_group[:, :, None] == group_ids[None, None, :]
    chosen = lax.optimization_barrier(jnp.sum(jnp.where(match_group, group_ids[None, :, None], 0), axis=1)).astype(jnp.int32)
    stacks = decoded_clips[group_ids[None, :], chosen.T]
    stacks = stacks.reshape(N_SEQ, STACK, F, COLS, C)
    starts = (jnp.cumsum(band_rows, axis=1) - band_rows).astype(jnp.int32)
    offsets = jnp.arange(BAND_MAX, dtype=jnp.int32)
    live_mask = offsets[None, None, :] < band_rows[:, :, None]
    pick_rows = jnp.where(live_mask, starts[:, :, None] + offsets[None, None, :], 0).astype(jnp.int32)
    pick_rows = pick_rows.reshape(N_SEQ, N_DEC * BAND_MAX)
    gathered = jax.vmap(lambda stack_one, pick_one: stack_one[pick_one])(stacks, pick_rows)
    gathered = gathered.reshape(N_SEQ, N_DEC, BAND_MAX, F, COLS, C)
    return jnp.where(live_mask[:, :, :, None, None, None], gathered, jnp.zeros((), jnp.bfloat16))
```

```python
import jax
import jax.numpy as jnp
from jax import lax
from jax.experimental import pallas as pl
from jax.experimental.pallas import tpu as pltpu
from jax.sharding import PartitionSpec as P

F = 4
CT = 2
COLS = 16
ZC = 16
C = 384
FRAMES = F + CT
PAD_FRAMES = 8
ROW = F * COLS
BAND = 24
EXT = BAND + 4
MID = BAND + 2
LANES = 128
EPSILON = 1e-06
MESH = pl.DeviceIdType.MESH


def band_start(band_rows, group, owner, owners):
    return lax.fori_loop(
        0,
        owners,
        lambda o, total: total + jnp.where(o < owner, band_rows[group, o], 0),
        jnp.int32(0),
    )


def exchange(
    clip_group,
    band_rows,
    lat,
    act,
    got_lat,
    got_act,
    clip_lat,
    clip_act,
    stack_lat,
    stack_act,
    slot_lat,
    slot_act,
    send_one,
    recv_one,
    send_two,
    recv_two,
):
    groups = lax.axis_size("seq")
    owners = lax.axis_size("dec")
    seq_at = lax.axis_index("seq")
    dec_at = lax.axis_index("dec")
    per_owner = lat.shape[1]

    barrier = pltpu.get_barrier_semaphore()
    for step in range(1, groups):
        pl.semaphore_signal(
            barrier,
            inc=1,
            device_id=(lax.rem(seq_at + step, groups), dec_at),
            device_id_type=MESH,
        )

    def greet(step, carry):
        pl.semaphore_signal(
            barrier,
            inc=1,
            device_id=(seq_at, lax.rem(dec_at + step, owners)),
            device_id_type=MESH,
        )
        return carry

    lax.fori_loop(1, owners, greet, 0)

    for group in range(groups):
        clip = jnp.int32(0)
        for i in range(groups):
            clip = clip + jnp.where(clip_group[seq_at, i] == group, i, 0)
        clip = jnp.minimum(clip, groups - 1)
        clip_lat[group] = lat[clip]
        clip_act[group] = act[clip]
    stack_lat[seq_at] = clip_lat[seq_at]
    stack_act[seq_at] = clip_act[seq_at]
    pl.semaphore_wait(barrier, groups - 1 + owners - 1)

    def to_group(step, which):
        group = lax.rem(seq_at + step, groups)
        source, target = ((clip_lat, stack_lat), (clip_act, stack_act))[which]
        return pltpu.make_async_remote_copy(
            src_ref=source.at[group],
            dst_ref=target.at[seq_at],
            send_sem=send_one.at[which, step],
            recv_sem=recv_one.at[which, step],
            device_id=(group, dec_at),
            device_id_type=MESH,
        )

    for which in range(2):
        for step in range(1, groups):
            to_group(step, which).start()

    def held_row(owner, start):
        first = lax.shift_right_arithmetic(start - 2 - dec_at + owners - 1, 5)
        return jnp.clip(first, 0, groups * per_owner - 1)

    def to_owner(step, which):
        owner = lax.rem(dec_at + step, owners)
        source, target = ((slot_lat, got_lat), (slot_act, got_act))[which]
        return pltpu.make_async_remote_copy(
            src_ref=source.at[owner],
            dst_ref=target.at[dec_at],
            send_sem=send_two.at[which, step],
            recv_sem=recv_two.at[which, step],
            device_id=(seq_at, owner),
            device_id_type=MESH,
        )

    for which in range(2):
        for step in range(1, groups):
            to_group(step, which).wait_recv()
        stack, slot, got = (
            (stack_lat, slot_lat, got_lat),
            (stack_act, slot_act, got_act),
        )[which]

        def fill(owner, start, stack=stack, slot=slot):
            row = held_row(owner, start)
            slot[owner] = stack[row // per_owner, lax.rem(row, per_owner)]
            return start + band_rows[seq_at, owner]

        lax.fori_loop(0, owners, fill, jnp.int32(0))
        got[dec_at] = slot[dec_at]

        def launch(step, carry, which=which):
            to_owner(step, which).start()
            return carry

        lax.fori_loop(1, owners, launch, 0)
    for which in range(2):
        for step in range(1, groups):
            to_group(step, which).wait_send()

        def finish(step, carry, which=which):
            to_owner(step, which).wait()
            return carry

        lax.fori_loop(1, owners, finish, 0)


def first_stage(start, got_lat, w_in, gain, wide, spread, taps, w_first, first_out):
    w_first[...] = jnp.zeros_like(w_first)
    for time_tap in range(3):
        for row_tap in range(3):
            at = row_tap * 256 + time_tap * 64
            w_first[at : at + 48, :] = w_in[time_tap * 3 + row_tap]

    lane = lax.broadcasted_iota(jnp.int32, (PAD_FRAMES, LANES), 1)
    spread[EXT] = jnp.zeros((PAD_FRAMES * COLS, LANES), jnp.float32)

    def columns(j, carry):
        frames = got_lat[(start - 2 + j) & 31].astype(jnp.float32)
        for col in range(COLS):
            turned = pltpu.roll(frames, (-(ZC * (col - 1))) % (COLS * ZC), 1)[:, :LANES]
            low = ZC if col == 0 else 0
            high = 2 * ZC if col == COLS - 1 else 3 * ZC
            keep = (lane >= low) & (lane < high)
            spread[j, pl.ds(col, PAD_FRAMES, stride=COLS), :] = jnp.where(keep, turned, 0.0)
        return carry

    lax.fori_loop(0, EXT, columns, 0)

    def pair(j, carry):
        here = spread[j]
        after = pltpu.roll(here, 64, 1)
        count = FRAMES * COLS
        taps[j] = (here[:count] + after[COLS : COLS + count]).astype(jnp.bfloat16)
        return carry

    lax.fori_loop(0, EXT + 1, pair, 0)

    rows = MID // 2
    for part in range(2):
        blocks = []
        for r in range(rows):
            j = part * rows + r + 1
            height = lax.rem(start - 2 + j + 96, 96)
            picks = (
                jnp.where(height == 0, EXT, j - 1),
                j,
                jnp.where(height == 95, EXT, j + 1),
            )
            pieces = []
            for pick in picks:
                block = taps[pick]
                pieces += [block[:ROW], block[2 * COLS : 2 * COLS + ROW]]
            blocks.append(jnp.concatenate(pieces, axis=1))
        slab = jnp.concatenate(blocks, axis=0)
        total = jnp.dot(slab, w_first[...], preferred_element_type=jnp.float32)
        first_out[part * rows : (part + 1) * rows] = total.reshape(rows, ROW, C)


def shifted(values, position):
    count = values.shape[0]
    before = jnp.where(position == 0, 0.0, pltpu.roll(values, 1, 0))
    after = jnp.where(position == COLS - 1, 0.0, pltpu.roll(values, count - 1, 0))
    return jnp.concatenate([before, values, after], axis=1).astype(jnp.bfloat16)


def cache_stage(start, got_act, conv_in):
    position = lax.broadcasted_iota(jnp.int32, (CT * COLS, C), 0) & (COLS - 1)

    def one(i, carry):
        values = got_act[(start - 1 + i) & 31].astype(jnp.float32)
        conv_in[i, : CT * COLS] = shifted(values, position)
        return carry

    lax.fori_loop(0, MID, one, 0)


def act_stage(gain, first_out, conv_in):
    position = lax.broadcasted_iota(jnp.int32, (ROW, C), 0) & (COLS - 1)
    conv_in[MID] = jnp.zeros((FRAMES * COLS, 3 * C), jnp.bfloat16)

    def one(i, carry):
        values = first_out[i]
        mean = jnp.mean(values * values, axis=1, keepdims=True)
        scaled = values * lax.rsqrt(mean + EPSILON) * gain[...]
        conv_in[i, CT * COLS :] = shifted(scaled / (1.0 + jnp.exp(-scaled)), position)
        return carry

    lax.fori_loop(0, MID, one, 0)


def second_stage(start, live, w_mid, first_out, conv_in, out, chunk):
    def rows_from(part, carry):
        base = part * chunk
        total = jnp.zeros((chunk * ROW, C), jnp.float32)
        for row_tap in range(3):
            picks = []
            for r in range(chunk):
                height = lax.rem(start + base + r, 96)
                pick = base + r + row_tap
                if row_tap == 0:
                    pick = jnp.where(height == 0, MID, pick)
                if row_tap == 2:
                    pick = jnp.where(height == 95, MID, pick)
                picks.append(pick)
            for time_tap in range(3):
                at = time_tap * COLS
                slab = jnp.concatenate(
                    [conv_in[pick, at : at + ROW, :] for pick in picks], axis=0
                )
                total = total + jnp.dot(
                    slab, w_mid[time_tap * 3 + row_tap], preferred_element_type=jnp.float32
                )
        for r in range(chunk):
            value = total[r * ROW : (r + 1) * ROW] + first_out[base + r + 1]
            out[base + r] = jnp.where(base + r < live, value, 0.0).astype(jnp.bfloat16)
        return carry

    lax.fori_loop(0, BAND // chunk, rows_from, 0)


def convolve(
    place,
    band_rows,
    got_lat,
    got_act,
    w_in,
    w_mid,
    gain,
    out,
    wide,
    spread,
    taps,
    w_first,
    first_out,
    conv_in,
):
    group, owner = place[0], place[1]
    start = band_start(band_rows, group, owner, band_rows.shape[1])
    live = band_rows[group, owner]
    cache_stage(start, got_act, conv_in)
    first_stage(start, got_lat, w_in, gain, wide, spread, taps, w_first, first_out)
    act_stage(gain, first_out, conv_in)
    second_stage(start, live, w_mid, first_out, conv_in, out, 8)


VM = pl.BlockSpec(memory_space=pltpu.VMEM)
SM = pl.BlockSpec(memory_space=pltpu.SMEM)


def run_convolve(place, band_rows, got_lat, got_act, w_in, w_mid, gain):
    return pl.pallas_call(
        convolve,
        out_shape=jax.ShapeDtypeStruct((BAND, ROW, C), jnp.bfloat16),
        in_specs=[SM, SM, VM, VM, VM, VM, VM],
        out_specs=VM,
        scratch_shapes=[
            pltpu.VMEM((8, 128), jnp.float32),
            pltpu.VMEM((EXT + 1, PAD_FRAMES * COLS, LANES), jnp.float32),
            pltpu.VMEM((EXT + 1, FRAMES * COLS, LANES), jnp.bfloat16),
            pltpu.VMEM((768, C), jnp.bfloat16),
            pltpu.VMEM((MID, ROW, C), jnp.float32),
            pltpu.VMEM((MID + 1, FRAMES * COLS, 3 * C), jnp.bfloat16),
        ],
        compiler_params=pltpu.CompilerParams(vmem_limit_bytes=48 << 20),
        name="convolve",
    )(place, band_rows, got_lat, got_act, w_in, w_mid, gain)


def run_exchange(clip_group, band_rows, lat, act):
    groups = lax.axis_size("seq")
    owners = lax.axis_size("dec")
    per_owner = lat.shape[1]
    lat_row, act_row = lat.shape[2:], act.shape[2:]
    bf16 = jnp.bfloat16
    return pl.pallas_call(
        exchange,
        out_shape=(
            jax.ShapeDtypeStruct((owners,) + lat_row, bf16),
            jax.ShapeDtypeStruct((owners,) + act_row, bf16),
        ),
        in_specs=[SM, SM, VM, VM],
        out_specs=(VM, VM),
        scratch_shapes=[
            pltpu.VMEM((groups, per_owner) + lat_row, bf16),
            pltpu.VMEM((groups, per_owner) + act_row, bf16),
            pltpu.VMEM((groups, per_owner) + lat_row, bf16),
            pltpu.VMEM((groups, per_owner) + act_row, bf16),
            pltpu.VMEM((owners,) + lat_row, bf16),
            pltpu.VMEM((owners,) + act_row, bf16),
            pltpu.SemaphoreType.DMA((2, groups)),
            pltpu.SemaphoreType.DMA((2, groups)),
            pltpu.SemaphoreType.DMA((2, owners)),
            pltpu.SemaphoreType.DMA((2, owners)),
        ],
        compiler_params=pltpu.CompilerParams(
            collective_id=0, has_side_effects=True, vmem_limit_bytes=16 << 20
        ),
        name="exchange",
    )(clip_group, band_rows, lat, act)


def shards(latents, cache_lat, cache_act, w_in, w_mid, norm_gain, clip_group, band_rows):
    groups, per_owner = latents.shape[1], latents.shape[2]
    new_lat = latents.reshape(groups, per_owner, F, COLS * ZC)
    old_lat = cache_lat.reshape(groups, per_owner, CT, COLS * ZC)
    lat = jnp.concatenate([old_lat, new_lat, jnp.zeros_like(old_lat)], axis=2)
    act = cache_act.reshape(groups, per_owner, CT * COLS, C)
    got_lat, got_act = run_exchange(clip_group, band_rows, lat, act)
    place = jnp.stack([lax.axis_index("seq"), lax.axis_index("dec")]).astype(jnp.int32)
    out = run_convolve(
        place,
        band_rows,
        got_lat,
        got_act,
        w_in.reshape(9, 3 * ZC, C),
        w_mid.reshape(9, 3 * C, C),
        norm_gain.reshape(1, C),
    )
    return out.reshape(1, 1, BAND, F, COLS, C)


def solution(mesh):
    placed = P("seq", None, None, "dec", None)
    return jax.shard_map(
        shards,
        mesh=mesh,
        in_specs=(placed, placed, placed, P(), P(), P(), P(), P()),
        out_specs=P("seq", "dec", None, None, None, None),
        check_vma=False,
    )
```

```python
import jax
import jax.numpy as jnp
from jax import lax
from jax.experimental import pallas as pl
from jax.experimental.pallas import tpu as pltpu
from jax.sharding import PartitionSpec as P

F = 4
CT = 2
COLS = 16
ZC = 16
C = 384
FRAMES = F + CT
PAD_FRAMES = 8
ROW = F * COLS
BAND = 24
EXT = BAND + 4
MID = BAND + 2
LANES = 128
EPSILON = 1e-06
MESH = pl.DeviceIdType.MESH


def band_start(band_rows, group, owner, owners):
    return lax.fori_loop(
        0,
        owners,
        lambda o, total: total + jnp.where(o < owner, band_rows[group, o], 0),
        jnp.int32(0),
    )


def first_stage(start, got_lat, spread, taps, w_first, first_out):
    lane = lax.broadcasted_iota(jnp.int32, (PAD_FRAMES, LANES), 1)
    spread[EXT] = jnp.zeros((PAD_FRAMES * COLS, LANES), jnp.float32)

    def columns(j, carry):
        frames = got_lat[(start - 2 + j) & 31].astype(jnp.float32)
        for col in range(COLS):
            turned = pltpu.roll(frames, (-(ZC * (col - 1))) % (COLS * ZC), 1)[:, :LANES]
            low = ZC if col == 0 else 0
            high = 2 * ZC if col == COLS - 1 else 3 * ZC
            keep = (lane >= low) & (lane < high)
            spread[j, pl.ds(col, PAD_FRAMES, stride=COLS), :] = jnp.where(keep, turned, 0.0)
        return carry

    lax.fori_loop(0, EXT, columns, 0)

    def pair(j, carry):
        here = spread[j]
        after = pltpu.roll(here, 64, 1)
        count = FRAMES * COLS
        taps[j] = (here[:count] + after[COLS : COLS + count]).astype(jnp.bfloat16)
        return carry

    lax.fori_loop(0, EXT + 1, pair, 0)

    rows = MID // 2
    for part in range(2):
        blocks = []
        for r in range(rows):
            j = part * rows + r + 1
            height = lax.rem(start - 2 + j + 96, 96)
            picks = (
                jnp.where(height == 0, EXT, j - 1),
                j,
                jnp.where(height == 95, EXT, j + 1),
            )
            pieces = []
            for pick in picks:
                block = taps[pick]
                pieces += [block[:ROW], block[2 * COLS : 2 * COLS + ROW]]
            blocks.append(jnp.concatenate(pieces, axis=1))
        slab = jnp.concatenate(blocks, axis=0)
        total = jnp.dot(slab, w_first[...], preferred_element_type=jnp.float32)
        first_out[part * rows : (part + 1) * rows] = total.reshape(rows, ROW, C)


def shifted(values, position):
    count = values.shape[0]
    before = jnp.where(position == 0, 0.0, pltpu.roll(values, 1, 0))
    after = jnp.where(position == COLS - 1, 0.0, pltpu.roll(values, count - 1, 0))
    return jnp.concatenate([before, values, after], axis=1).astype(jnp.bfloat16)


def cache_stage(start, got_act, conv_in):
    position = lax.broadcasted_iota(jnp.int32, (CT * COLS, C), 0) & (COLS - 1)

    def one(i, carry):
        values = got_act[(start - 1 + i) & 31].astype(jnp.float32)
        conv_in[i, : CT * COLS] = shifted(values, position)
        return carry

    lax.fori_loop(0, MID, one, 0)


def act_stage(gain, first_out, conv_in):
    position = lax.broadcasted_iota(jnp.int32, (ROW, C), 0) & (COLS - 1)
    conv_in[MID] = jnp.zeros((FRAMES * COLS, 3 * C), jnp.bfloat16)

    def one(i, carry):
        values = first_out[i]
        mean = jnp.mean(values * values, axis=1, keepdims=True)
        scaled = values * lax.rsqrt(mean + EPSILON) * gain[...]
        conv_in[i, CT * COLS :] = shifted(scaled / (1.0 + jnp.exp(-scaled)), position)
        return carry

    lax.fori_loop(0, MID, one, 0)


def tap_rows(start, row):
    height = lax.rem(start + row, 96)
    return (
        jnp.where(height == 0, MID, row),
        row + 1,
        jnp.where(height == 95, MID, row + 2),
    )


def tap_sum(start, base, count, time_tap, low, high, w_mid, conv_in):
    at = (low + time_tap) * COLS
    size = (high - low) * COLS
    blocks = []
    for r in range(count):
        picks = tap_rows(start, base + r)
        blocks.append(
            jnp.concatenate([conv_in[pick, at : at + size, :] for pick in picks], axis=1)
        )
    slab = jnp.concatenate(blocks, axis=0)
    return jnp.dot(slab, w_mid[time_tap], preferred_element_type=jnp.float32)


def second_new(start, w_mid, first_out, conv_in, chunk):
    def some(part, carry):
        base = part * chunk
        for time_tap in range(3):
            low = CT - time_tap
            size = (F - low) * COLS
            total = tap_sum(start, base, chunk, time_tap, low, F, w_mid, conv_in)
            for r in range(chunk):
                first_out[base + r + 1, low * COLS :] += total[r * size : (r + 1) * size]
        return carry

    lax.fori_loop(0, BAND // chunk, some, 0)


def second_old(start, live, w_mid, first_out, conv_in, out, chunk):
    def some(part, carry):
        base = part * chunk
        for time_tap in range(CT):
            size = (CT - time_tap) * COLS
            total = tap_sum(start, base, chunk, time_tap, 0, CT - time_tap, w_mid, conv_in)
            for r in range(chunk):
                first_out[base + r + 1, :size] += total[r * size : (r + 1) * size]
        for r in range(chunk):
            value = first_out[base + r + 1]
            out[base + r] = jnp.where(base + r < live, value, 0.0).astype(jnp.bfloat16)
        return carry

    lax.fori_loop(0, BAND // chunk, some, 0)


def block(
    clip_group,
    band_rows,
    lat,
    act,
    gain,
    w_in,
    w_mid,
    out,
    got_lat,
    got_act,
    clip_lat,
    clip_act,
    stack_lat,
    stack_act,
    slot_lat,
    slot_act,
    w_first,
    w_second,
    spread,
    taps,
    first_out,
    conv_in,
    send_one,
    recv_one,
    send_two,
    recv_two,
    load,
):
    groups = lax.axis_size("seq")
    owners = lax.axis_size("dec")
    seq_at = lax.axis_index("seq")
    dec_at = lax.axis_index("dec")
    per_owner = lat.shape[1]

    barrier = pltpu.get_barrier_semaphore()
    for step in range(1, groups):
        pl.semaphore_signal(
            barrier,
            inc=1,
            device_id=(lax.rem(seq_at + step, groups), dec_at),
            device_id_type=MESH,
        )

    def greet(step, carry):
        pl.semaphore_signal(
            barrier,
            inc=1,
            device_id=(seq_at, lax.rem(dec_at + step, owners)),
            device_id_type=MESH,
        )
        return carry

    lax.fori_loop(1, owners, greet, 0)

    for group in range(groups):
        clip = jnp.int32(0)
        for i in range(groups):
            clip = clip + jnp.where(clip_group[seq_at, i] == group, i, 0)
        clip = jnp.minimum(clip, groups - 1)
        clip_lat[group] = lat[clip]
        clip_act[group] = act[clip]
    stack_lat[seq_at] = clip_lat[seq_at]
    stack_act[seq_at] = clip_act[seq_at]
    w_first[...] = jnp.zeros_like(w_first)
    pl.semaphore_wait(barrier, groups - 1 + owners - 1)

    def to_group(step, which):
        group = lax.rem(seq_at + step, groups)
        source, target = ((clip_lat, stack_lat), (clip_act, stack_act))[which]
        return pltpu.make_async_remote_copy(
            src_ref=source.at[group],
            dst_ref=target.at[seq_at],
            send_sem=send_one.at[which, step],
            recv_sem=recv_one.at[which, step],
            device_id=(group, dec_at),
            device_id_type=MESH,
        )

    for which in range(2):
        for step in range(1, groups):
            to_group(step, which).start()

    loads = [pltpu.make_async_copy(w_mid, w_second, load.at[9])]
    for time_tap in range(3):
        for row_tap in range(3):
            tap = time_tap * 3 + row_tap
            at = row_tap * 256 + time_tap * 64
            loads.append(
                pltpu.make_async_copy(
                    w_in.at[tap], w_first.at[at : at + 3 * ZC, :], load.at[tap]
                )
            )
    for copy in loads[1:] + loads[:1]:
        copy.start()

    def held_row(owner, start):
        first = lax.shift_right_arithmetic(start - 2 - dec_at + owners - 1, 5)
        return jnp.clip(first, 0, groups * per_owner - 1)

    def to_owner(step, which):
        owner = lax.rem(dec_at + step, owners)
        source, target = ((slot_lat, got_lat), (slot_act, got_act))[which]
        return pltpu.make_async_remote_copy(
            src_ref=source.at[owner],
            dst_ref=target.at[dec_at],
            send_sem=send_two.at[which, step],
            recv_sem=recv_two.at[which, step],
            device_id=(seq_at, owner),
            device_id_type=MESH,
        )

    def pass_on(which):
        stack, slot, got = (
            (stack_lat, slot_lat, got_lat),
            (stack_act, slot_act, got_act),
        )[which]
        for step in range(1, groups):
            to_group(step, which).wait_recv()

        def fill(owner, start):
            row = held_row(owner, start)
            slot[owner] = stack[row // per_owner, lax.rem(row, per_owner)]
            return start + band_rows[seq_at, owner]

        lax.fori_loop(0, owners, fill, jnp.int32(0))
        got[dec_at] = slot[dec_at]

        def launch(step, carry):
            to_owner(step, which).start()
            return carry

        lax.fori_loop(1, owners, launch, 0)

    def collect(which):
        def arrive(step, carry):
            to_owner(step, which).wait_recv()
            return carry

        lax.fori_loop(1, owners, arrive, 0)

    start = band_start(band_rows, seq_at, dec_at, owners)
    live = band_rows[seq_at, dec_at]
    pass_on(0)
    pass_on(1)
    collect(0)
    for copy in loads[1:]:
        copy.wait()
    first_stage(start, got_lat, spread, taps, w_first, first_out)
    act_stage(gain, first_out, conv_in)
    loads[0].wait()
    second_new(start, w_second, first_out, conv_in, 8)
    collect(1)
    cache_stage(start, got_act, conv_in)
    second_old(start, live, w_second, first_out, conv_in, out, 24)

    for which in range(2):
        for step in range(1, groups):
            to_group(step, which).wait_send()

        def finish(step, carry, which=which):
            to_owner(step, which).wait_send()
            return carry

        lax.fori_loop(1, owners, finish, 0)


def run_block(clip_group, band_rows, lat, act, gain, w_in, w_mid):
    groups = lax.axis_size("seq")
    owners = lax.axis_size("dec")
    per_owner = lat.shape[1]
    lat_row, act_row = lat.shape[2:], act.shape[2:]
    bf16 = jnp.bfloat16
    vm = pl.BlockSpec(memory_space=pltpu.VMEM)
    sm = pl.BlockSpec(memory_space=pltpu.SMEM)
    hbm = pl.BlockSpec(memory_space=pl.ANY)
    return pl.pallas_call(
        block,
        out_shape=jax.ShapeDtypeStruct((BAND, ROW, C), bf16),
        in_specs=[sm, sm, vm, vm, vm, hbm, hbm],
        out_specs=vm,
        scratch_shapes=[
            pltpu.VMEM((owners,) + lat_row, bf16),
            pltpu.VMEM((owners,) + act_row, bf16),
            pltpu.VMEM((groups, per_owner) + lat_row, bf16),
            pltpu.VMEM((groups, per_owner) + act_row, bf16),
            pltpu.VMEM((groups, per_owner) + lat_row, bf16),
            pltpu.VMEM((groups, per_owner) + act_row, bf16),
            pltpu.VMEM((owners,) + lat_row, bf16),
            pltpu.VMEM((owners,) + act_row, bf16),
            pltpu.VMEM((768, C), bf16),
            pltpu.VMEM(w_mid.shape, bf16),
            pltpu.VMEM((EXT + 1, PAD_FRAMES * COLS, LANES), jnp.float32),
            pltpu.VMEM((EXT + 1, FRAMES * COLS, LANES), bf16),
            pltpu.VMEM((MID, ROW, C), jnp.float32),
            pltpu.VMEM((MID + 1, FRAMES * COLS, 3 * C), bf16),
            pltpu.SemaphoreType.DMA((2, groups)),
            pltpu.SemaphoreType.DMA((2, groups)),
            pltpu.SemaphoreType.DMA((2, owners)),
            pltpu.SemaphoreType.DMA((2, owners)),
            pltpu.SemaphoreType.DMA((10,)),
        ],
        compiler_params=pltpu.CompilerParams(
            collective_id=0, has_side_effects=True, vmem_limit_bytes=52 << 20
        ),
        name="block",
    )(clip_group, band_rows, lat, act, gain, w_in, w_mid)


def shards(latents, cache_lat, cache_act, w_in, w_mid, norm_gain, clip_group, band_rows):
    groups, per_owner = latents.shape[1], latents.shape[2]
    new_lat = latents.reshape(groups, per_owner, F, COLS * ZC)
    old_lat = cache_lat.reshape(groups, per_owner, CT, COLS * ZC)
    lat = jnp.concatenate([old_lat, new_lat, jnp.zeros_like(old_lat)], axis=2)
    act = cache_act.reshape(groups, per_owner, CT * COLS, C)
    out = run_block(
        clip_group,
        band_rows,
        lat,
        act,
        norm_gain.reshape(1, C),
        w_in.reshape(9, 3 * ZC, C),
        w_mid.reshape(3, 9 * C, C),
    )
    return out.reshape(1, 1, BAND, F, COLS, C)


def solution(mesh):
    placed = P("seq", None, None, "dec", None)
    return jax.shard_map(
        shards,
        mesh=mesh,
        in_specs=(placed, placed, placed, P(), P(), P(), P(), P()),
        out_specs=P("seq", "dec", None, None, None, None),
        check_vma=False,
    )
```

```python
import jax
import jax.numpy as jnp
from jax import lax
from jax.experimental import pallas as pl
from jax.experimental.pallas import tpu as pltpu
from jax.sharding import PartitionSpec as P

F = 4
CT = 2
COLS = 16
ZC = 16
C = 384
FRAMES = F + CT
PAD_FRAMES = 8
ROW = F * COLS
BAND = 24
EXT = BAND + 4
MID = BAND + 2
LANES = 128
TOGETHER = 4
EPSILON = 1e-06
MESH = pl.DeviceIdType.MESH


def band_start(band_rows, group, owner, owners):
    return lax.fori_loop(
        0,
        owners,
        lambda o, total: total + jnp.where(o < owner, band_rows[group, o], 0),
        jnp.int32(0),
    )


def make_pick(pick):
    shape = (2 * COLS * ZC, LANES)
    source = lax.broadcasted_iota(jnp.int32, shape, 0)
    lane = lax.broadcasted_iota(jnp.int32, shape, 1)
    frame = source >= COLS * ZC
    inner = jnp.where(frame, lane - 64, lane)
    here = source & (COLS * ZC - 1)

    inside = (inner >= 0) & (inner < 3 * ZC)

    def some(part, carry):
        for i in range(TOGETHER):
            wanted = here - ZC * (part * TOGETHER + i - 1)
            block = jnp.where(inside & (inner == wanted), 1.0, 0.0).astype(jnp.bfloat16)
            pick[part, :, i * LANES : (i + 1) * LANES] = block
        return carry

    lax.fori_loop(0, COLS // TOGETHER, some, 0)


def first_stage(start, got_lat, pick, pairs, spread, taps, w_first, first_out):
    def gather(i, carry):
        rows = []
        for k in range(2):
            frames = got_lat[(start - 2 + 2 * i + k) & 31].astype(jnp.float32)
            after = pltpu.roll(frames, PAD_FRAMES - 1, 0)
            rows.append(jnp.concatenate([frames, after], axis=1))
        pairs[i] = jnp.concatenate(rows, axis=0).astype(jnp.bfloat16)
        return carry

    lax.fori_loop(0, EXT // 2, gather, 0)
    source = pairs[...].reshape(EXT * PAD_FRAMES, 2 * COLS * ZC)

    def columns(part, carry):
        block = jnp.dot(source, pick[part], preferred_element_type=jnp.float32)
        for i in range(TOGETHER):
            col = part * TOGETHER + i
            rows = pl.ds(col, EXT * PAD_FRAMES, stride=COLS)
            spread[rows, :] = block[:, i * LANES : (i + 1) * LANES]
        return carry

    lax.fori_loop(0, COLS // TOGETHER, columns, 0)
    taps[EXT] = jnp.zeros((FRAMES * COLS, LANES), jnp.bfloat16)

    def narrow(j, carry):
        at = pl.multiple_of(j * PAD_FRAMES * COLS, PAD_FRAMES * COLS)
        taps[j] = spread[pl.ds(at, FRAMES * COLS), :].astype(jnp.bfloat16)
        return carry

    lax.fori_loop(0, EXT, narrow, 0)

    rows = MID // 2
    for part in range(2):
        blocks = []
        for r in range(rows):
            j = part * rows + r + 1
            height = lax.rem(start - 2 + j + 96, 96)
            picks = (
                jnp.where(height == 0, EXT, j - 1),
                j,
                jnp.where(height == 95, EXT, j + 1),
            )
            pieces = []
            for at in picks:
                block = taps[at]
                pieces += [block[:ROW], block[2 * COLS : 2 * COLS + ROW]]
            blocks.append(jnp.concatenate(pieces, axis=1))
        slab = jnp.concatenate(blocks, axis=0)
        total = jnp.dot(slab, w_first[...], preferred_element_type=jnp.float32)
        first_out[part * rows : (part + 1) * rows] = total.reshape(rows, ROW, C)


def shifted(values, position):
    count = values.shape[0]
    before = jnp.where(position == 0, 0.0, pltpu.roll(values, 1, 0))
    after = jnp.where(position == COLS - 1, 0.0, pltpu.roll(values, count - 1, 0))
    return jnp.concatenate([before, values, after], axis=1).astype(jnp.bfloat16)


def cache_stage(start, got_act, conv_in):
    position = lax.broadcasted_iota(jnp.int32, (CT * COLS, C), 0) & (COLS - 1)

    def one(i, carry):
        values = got_act[(start - 1 + i) & 31].astype(jnp.float32)
        conv_in[i, : CT * COLS] = shifted(values, position)
        return carry

    lax.fori_loop(0, MID, one, 0)


def act_stage(gain, first_out, conv_in):
    position = lax.broadcasted_iota(jnp.int32, (ROW, C), 0) & (COLS - 1)
    conv_in[MID] = jnp.zeros((FRAMES * COLS, 3 * C), jnp.bfloat16)
    half_gain = 0.5 * gain[...].reshape(1, C)

    def one(i, carry):
        values = first_out[i]
        mean = jnp.mean(values * values, axis=1, keepdims=True)
        half = values * lax.rsqrt(mean + EPSILON) * half_gain
        conv_in[i, CT * COLS :] = shifted(half + half * jnp.tanh(half), position)
        return carry

    lax.fori_loop(0, MID, one, 0)


def tap_rows(start, row):
    height = lax.rem(start + row, 96)
    return (
        jnp.where(height == 0, MID, row),
        row + 1,
        jnp.where(height == 95, MID, row + 2),
    )


def frame_sum(start, base, count, frame, frames, low, high, w_mid, conv_in):
    at = frame * COLS
    size = frames * COLS
    blocks = []
    for r in range(count):
        picks = tap_rows(start, base + r)
        blocks.append(
            jnp.concatenate([conv_in[at_row, at : at + size, :] for at_row in picks], axis=1)
        )
    slab = jnp.concatenate(blocks, axis=0)
    return jnp.dot(slab, w_mid[:, low * C : high * C], preferred_element_type=jnp.float32)


def spread_sum(base, count, frame, frames, low, high, total, first_out):
    size = frames * COLS
    for r in range(count):
        for tap in range(low, high):
            at = (frame - tap) * COLS
            part = total[r * size : (r + 1) * size, (tap - low) * C : (tap - low + 1) * C]
            first_out[base + r + 1, at : at + size] += part


NEW_FRAMES = ((2, 2, 0, 3), (4, 1, 1, 3), (5, 1, 2, 3))
OLD_FRAMES = ((1, 1, 0, 2), (0, 1, 0, 1))


def second_new(start, w_mid, first_out, conv_in, chunk):
    def some(part, carry):
        base = part * chunk
        for frame, frames, low, high in NEW_FRAMES:
            total = frame_sum(start, base, chunk, frame, frames, low, high, w_mid, conv_in)
            spread_sum(base, chunk, frame, frames, low, high, total, first_out)
        return carry

    lax.fori_loop(0, BAND // chunk, some, 0)


def second_old(start, live, w_mid, first_out, conv_in, out, chunk):
    def some(part, carry):
        base = part * chunk
        for frame, frames, low, high in OLD_FRAMES:
            total = frame_sum(start, base, chunk, frame, frames, low, high, w_mid, conv_in)
            spread_sum(base, chunk, frame, frames, low, high, total, first_out)
        for r in range(chunk):
            value = first_out[base + r + 1]
            out[base + r] = jnp.where(base + r < live, value, 0.0).astype(jnp.bfloat16)
        return carry

    lax.fori_loop(0, BAND // chunk, some, 0)


def block(
    clip_group,
    band_rows,
    new_lat,
    old_lat,
    old_act,
    gain,
    w_in,
    w_mid,
    out,
    raw_new,
    raw_old,
    raw_act,
    rows_lat,
    rows_act,
    pick,
    pairs,
    got_lat,
    got_act,
    clip_lat,
    clip_act,
    stack_lat,
    stack_act,
    slot_lat,
    slot_act,
    w_first,
    w_second,
    spread,
    taps,
    first_out,
    conv_in,
    send_one,
    recv_one,
    send_two,
    recv_two,
    load,
):
    groups = lax.axis_size("seq")
    owners = lax.axis_size("dec")
    seq_at = lax.axis_index("seq")
    dec_at = lax.axis_index("dec")
    per_owner = new_lat.shape[0]

    raw = [
        pltpu.make_async_copy(new_lat, raw_new, load.at[12]),
        pltpu.make_async_copy(old_lat, raw_old, load.at[13]),
        pltpu.make_async_copy(old_act, raw_act, load.at[14]),
    ]
    for copy in raw:
        copy.start()

    barrier = pltpu.get_barrier_semaphore()
    for step in range(1, groups):
        pl.semaphore_signal(
            barrier,
            inc=1,
            device_id=(lax.rem(seq_at + step, groups), dec_at),
            device_id_type=MESH,
        )

    def greet(step, carry):
        pl.semaphore_signal(
            barrier,
            inc=1,
            device_id=(seq_at, lax.rem(dec_at + step, owners)),
            device_id_type=MESH,
        )
        return carry

    lax.fori_loop(1, owners, greet, 0)

    for copy in raw:
        copy.wait()
    wide = COLS * ZC
    flat_lat = rows_lat.reshape(per_owner, wide // LANES, groups * PAD_FRAMES, LANES)
    flat_act = rows_act.reshape(per_owner, C // LANES, groups * CT * COLS, LANES)
    for t in range(per_owner):
        values = raw_old[t].astype(jnp.float32)
        for frame in range(CT):
            at = pl.ds(frame, groups, stride=PAD_FRAMES)
            for k in range(wide // LANES):
                lane = frame * wide + k * LANES
                flat_lat[t, k, at, :] = values[:, lane : lane + LANES]
        values = raw_new[t].astype(jnp.float32)
        for frame in range(F):
            at = pl.ds(CT + frame, groups, stride=PAD_FRAMES)
            for k in range(wide // LANES):
                lane = frame * wide + k * LANES
                flat_lat[t, k, at, :] = values[:, lane : lane + LANES]
        for frame in range(FRAMES, PAD_FRAMES):
            at = pl.ds(frame, groups, stride=PAD_FRAMES)
            for k in range(wide // LANES):
                flat_lat[t, k, at, :] = jnp.zeros((groups, LANES), jnp.float32)
        for q in range(CT * COLS):
            values = raw_act[t, :, q * C : (q + 1) * C].astype(jnp.float32)
            at = pl.ds(q, groups, stride=CT * COLS)
            for k in range(C // LANES):
                flat_act[t, k, at, :] = values[:, k * LANES : (k + 1) * LANES]

    for group in range(groups):
        clip = jnp.int32(0)
        for i in range(groups):
            clip = clip + jnp.where(clip_group[seq_at, i] == group, i, 0)
        clip = jnp.minimum(clip, groups - 1)
        for t in range(per_owner):
            parts = [rows_lat[t, k, clip] for k in range(wide // LANES)]
            clip_lat[group, t] = jnp.concatenate(parts, axis=1).astype(jnp.bfloat16)
            parts = [rows_act[t, k, clip] for k in range(C // LANES)]
            clip_act[group, t] = jnp.concatenate(parts, axis=1).astype(jnp.bfloat16)
    stack_lat[seq_at] = clip_lat[seq_at]
    stack_act[seq_at] = clip_act[seq_at]
    w_first[...] = jnp.zeros_like(w_first)
    make_pick(pick)
    pl.semaphore_wait(barrier, groups - 1 + owners - 1)

    def to_group(step, which):
        group = lax.rem(seq_at + step, groups)
        source, target = ((clip_lat, stack_lat), (clip_act, stack_act))[which]
        return pltpu.make_async_remote_copy(
            src_ref=source.at[group],
            dst_ref=target.at[seq_at],
            send_sem=send_one.at[which, step],
            recv_sem=recv_one.at[which, step],
            device_id=(group, dec_at),
            device_id_type=MESH,
        )

    for which in range(2):
        for step in range(1, groups):
            to_group(step, which).start()

    loads = [
        pltpu.make_async_copy(
            w_mid.at[tap], w_second.at[:, tap * C : (tap + 1) * C], load.at[9 + tap]
        )
        for tap in range(3)
    ]
    for time_tap in range(3):
        for row_tap in range(3):
            tap = time_tap * 3 + row_tap
            at = row_tap * 256 + time_tap * 64
            loads.append(
                pltpu.make_async_copy(
                    w_in.at[tap], w_first.at[at : at + 3 * ZC, :], load.at[tap]
                )
            )
    for copy in loads[3:] + loads[:3]:
        copy.start()

    def held_row(owner, start):
        first = lax.shift_right_arithmetic(start - 2 - dec_at + owners - 1, 5)
        return jnp.clip(first, 0, groups * per_owner - 1)

    def to_owner(step, which):
        owner = lax.rem(dec_at + step, owners)
        source, target = ((slot_lat, got_lat), (slot_act, got_act))[which]
        return pltpu.make_async_remote_copy(
            src_ref=source.at[owner],
            dst_ref=target.at[dec_at],
            send_sem=send_two.at[which, step],
            recv_sem=recv_two.at[which, step],
            device_id=(seq_at, owner),
            device_id_type=MESH,
        )

    def pass_on(which):
        stack, slot, got = (
            (stack_lat, slot_lat, got_lat),
            (stack_act, slot_act, got_act),
        )[which]
        for step in range(1, groups):
            to_group(step, which).wait_recv()

        def fill(owner, start):
            row = held_row(owner, start)
            slot[owner] = stack[row // per_owner, lax.rem(row, per_owner)]
            return start + band_rows[seq_at, owner]

        lax.fori_loop(0, owners, fill, jnp.int32(0))
        got[dec_at] = slot[dec_at]

        def launch(step, carry):
            to_owner(step, which).start()
            return carry

        lax.fori_loop(1, owners, launch, 0)

    def collect(which):
        def arrive(step, carry):
            to_owner(step, which).wait_recv()
            return carry

        lax.fori_loop(1, owners, arrive, 0)

    start = band_start(band_rows, seq_at, dec_at, owners)
    live = band_rows[seq_at, dec_at]
    pass_on(0)
    pass_on(1)
    collect(0)
    for copy in loads[3:]:
        copy.wait()
    first_stage(start, got_lat, pick, pairs, spread, taps, w_first, first_out)
    act_stage(gain, first_out, conv_in)
    for copy in loads[:3]:
        copy.wait()
    second_new(start, w_second, first_out, conv_in, 12)
    collect(1)
    cache_stage(start, got_act, conv_in)
    second_old(start, live, w_second, first_out, conv_in, out, 24)

    for which in range(2):
        for step in range(1, groups):
            to_group(step, which).wait_send()

        def finish(step, carry, which=which):
            to_owner(step, which).wait_send()
            return carry

        lax.fori_loop(1, owners, finish, 0)


def run_block(clip_group, band_rows, new_lat, old_lat, old_act, gain, w_in, w_mid):
    groups = lax.axis_size("seq")
    owners = lax.axis_size("dec")
    per_owner = new_lat.shape[0]
    lat_row, act_row = (PAD_FRAMES, COLS * ZC), (CT * COLS, C)
    bf16 = jnp.bfloat16
    vm = pl.BlockSpec(memory_space=pltpu.VMEM)
    sm = pl.BlockSpec(memory_space=pltpu.SMEM)
    hbm = pl.BlockSpec(memory_space=pl.ANY)
    return pl.pallas_call(
        block,
        out_shape=jax.ShapeDtypeStruct((BAND, ROW, C), bf16),
        in_specs=[sm, sm, hbm, hbm, hbm, vm, hbm, hbm],
        out_specs=vm,
        scratch_shapes=[
            pltpu.VMEM(new_lat.shape, bf16),
            pltpu.VMEM(old_lat.shape, bf16),
            pltpu.VMEM(old_act.shape, bf16),
            pltpu.VMEM((per_owner, COLS * ZC // LANES, groups, PAD_FRAMES, LANES), jnp.float32),
            pltpu.VMEM((per_owner, C // LANES, groups, CT * COLS, LANES), jnp.float32),
            pltpu.VMEM((COLS // TOGETHER, 2 * COLS * ZC, TOGETHER * LANES), bf16),
            pltpu.VMEM((EXT // 2, 2 * PAD_FRAMES, 2 * COLS * ZC), bf16),
            pltpu.VMEM((owners,) + lat_row, bf16),
            pltpu.VMEM((owners,) + act_row, bf16),
            pltpu.VMEM((groups, per_owner) + lat_row, bf16),
            pltpu.VMEM((groups, per_owner) + act_row, bf16),
            pltpu.VMEM((groups, per_owner) + lat_row, bf16),
            pltpu.VMEM((groups, per_owner) + act_row, bf16),
            pltpu.VMEM((owners,) + lat_row, bf16),
            pltpu.VMEM((owners,) + act_row, bf16),
            pltpu.VMEM((768, C), bf16),
            pltpu.VMEM((9 * C, 3 * C), bf16),
            pltpu.VMEM((EXT * PAD_FRAMES * COLS, LANES), jnp.float32),
            pltpu.VMEM((EXT + 1, FRAMES * COLS, LANES), bf16),
            pltpu.VMEM((MID, ROW, C), jnp.float32),
            pltpu.VMEM((MID + 1, FRAMES * COLS, 3 * C), bf16),
            pltpu.SemaphoreType.DMA((2, groups)),
            pltpu.SemaphoreType.DMA((2, groups)),
            pltpu.SemaphoreType.DMA((2, owners)),
            pltpu.SemaphoreType.DMA((2, owners)),
            pltpu.SemaphoreType.DMA((15,)),
        ],
        compiler_params=pltpu.CompilerParams(
            collective_id=0, has_side_effects=True, vmem_limit_bytes=56 << 20
        ),
        name="block",
    )(clip_group, band_rows, new_lat, old_lat, old_act, gain, w_in, w_mid)


def shards(latents, cache_lat, cache_act, w_in, w_mid, norm_gain, clip_group, band_rows):
    def by_time(rows):
        return jnp.transpose(rows[0, :, :, 0, :], (1, 0, 2))

    out = run_block(
        clip_group,
        band_rows,
        by_time(latents),
        by_time(cache_lat),
        by_time(cache_act),
        norm_gain,
        w_in.reshape(9, 3 * ZC, C),
        w_mid.reshape(3, 9 * C, C),
    )
    return out.reshape(1, 1, BAND, F, COLS, C)


def solution(mesh):
    placed = P("seq", None, None, "dec", None)
    return jax.shard_map(
        shards,
        mesh=mesh,
        in_specs=(placed, placed, placed, P(), P(), P(), P(), P()),
        out_specs=P("seq", "dec", None, None, None, None),
        check_vma=False,
    )
```

```python
import jax
import jax.numpy as jnp
from jax import lax
from jax.experimental import pallas as pl
from jax.experimental.pallas import tpu as pltpu
from jax.sharding import PartitionSpec as P

F = 4
CT = 2
COLS = 16
ZC = 16
C = 384
FRAMES = F + CT
PAD_FRAMES = 8
ROW = F * COLS
BAND = 24
EXT = BAND + 4
MID = BAND + 2
LANES = 128
TOGETHER = 4
EPSILON = 1e-06
MESH = pl.DeviceIdType.MESH


def band_start(band_rows, group, owner, owners):
    return lax.fori_loop(
        0,
        owners,
        lambda o, total: total + jnp.where(o < owner, band_rows[group, o], 0),
        jnp.int32(0),
    )


def make_pick(pick):
    shape = (2 * COLS * ZC, LANES)
    source = lax.broadcasted_iota(jnp.int32, shape, 0)
    lane = lax.broadcasted_iota(jnp.int32, shape, 1)
    frame = source >= COLS * ZC
    inner = jnp.where(frame, lane - 64, lane)
    here = source & (COLS * ZC - 1)

    inside = (inner >= 0) & (inner < 3 * ZC)

    def some(part, carry):
        for i in range(TOGETHER):
            wanted = here - ZC * (part * TOGETHER + i - 1)
            block = jnp.where(inside & (inner == wanted), 1.0, 0.0).astype(jnp.bfloat16)
            pick[part, :, i * LANES : (i + 1) * LANES] = block
        return carry

    lax.fori_loop(0, COLS // TOGETHER, some, 0)


def first_stage(start, got_lat, pick, pairs, spread, taps, w_first, first_out):
    def gather(i, carry):
        rows = []
        for k in range(2):
            frames = got_lat[(start - 2 + 2 * i + k) & 31].astype(jnp.float32)
            after = pltpu.roll(frames, PAD_FRAMES - 1, 0)
            rows.append(jnp.concatenate([frames, after], axis=1))
        pairs[i] = jnp.concatenate(rows, axis=0).astype(jnp.bfloat16)
        return carry

    lax.fori_loop(0, EXT // 2, gather, 0)
    source = pairs[...].reshape(EXT * PAD_FRAMES, 2 * COLS * ZC)

    def columns(part, carry):
        block = jnp.dot(source, pick[part], preferred_element_type=jnp.float32)
        for i in range(TOGETHER):
            col = part * TOGETHER + i
            rows = pl.ds(col, EXT * PAD_FRAMES, stride=COLS)
            spread[rows, :] = block[:, i * LANES : (i + 1) * LANES]
        return carry

    lax.fori_loop(0, COLS // TOGETHER, columns, 0)
    taps[EXT] = jnp.zeros((FRAMES * COLS, LANES), jnp.bfloat16)

    def narrow(j, carry):
        at = pl.multiple_of(j * PAD_FRAMES * COLS, PAD_FRAMES * COLS)
        taps[j] = spread[pl.ds(at, FRAMES * COLS), :].astype(jnp.bfloat16)
        return carry

    lax.fori_loop(0, EXT, narrow, 0)

    rows = MID // 2
    for part in range(2):
        blocks = []
        for r in range(rows):
            j = part * rows + r + 1
            height = lax.rem(start - 2 + j + 96, 96)
            picks = (
                jnp.where(height == 0, EXT, j - 1),
                j,
                jnp.where(height == 95, EXT, j + 1),
            )
            pieces = []
            for at in picks:
                block = taps[at]
                pieces += [block[:ROW], block[2 * COLS : 2 * COLS + ROW]]
            blocks.append(jnp.concatenate(pieces, axis=1))
        slab = jnp.concatenate(blocks, axis=0)
        total = jnp.dot(slab, w_first[...], preferred_element_type=jnp.float32)
        first_out[part * rows : (part + 1) * rows] = total.reshape(rows, ROW, C)


def shifted(values, position):
    count = values.shape[0]
    before = jnp.where(position == 0, 0.0, pltpu.roll(values, 1, 0))
    after = jnp.where(position == COLS - 1, 0.0, pltpu.roll(values, count - 1, 0))
    return jnp.concatenate([before, values, after], axis=1).astype(jnp.bfloat16)


HALF = BAND // 2
SPAN = HALF + 2


def act_row(row, gain, first_out, position):
    values = first_out[row]
    mean = jnp.mean(values * values, axis=1, keepdims=True)
    half = values * lax.rsqrt(mean + EPSILON) * gain
    return shifted(half + half * jnp.tanh(half), position)


def act_first(gain, first_out, conv_a, conv_b):
    position = lax.broadcasted_iota(jnp.int32, (ROW, C), 0) & (COLS - 1)
    half_gain = 0.5 * gain[...].reshape(1, C)
    zero = jnp.zeros((FRAMES * COLS, 3 * C), jnp.bfloat16)
    conv_a[SPAN] = zero
    conv_b[SPAN] = zero

    def one(i, carry):
        conv_a[i, CT * COLS :] = act_row(i, half_gain, first_out, position)
        return carry

    lax.fori_loop(0, SPAN, one, 0)
    for i in range(2):
        conv_b[i, CT * COLS :] = conv_a[HALF + i, CT * COLS :]


def cache_stage(start, got_act, conv_a, conv_b):
    position = lax.broadcasted_iota(jnp.int32, (CT * COLS, C), 0) & (COLS - 1)

    def one(i, carry):
        for half, conv in enumerate((conv_a, conv_b)):
            at = start - 1 + i + half * HALF
            values = got_act[at & 31].astype(jnp.float32)
            conv[i, : CT * COLS] = shifted(values, position)
        return carry

    lax.fori_loop(0, SPAN, one, 0)


def tap_rows(start, half, row):
    height = lax.rem(start + half * HALF + row, 96)
    return (
        jnp.where(height == 0, SPAN, row),
        row + 1,
        jnp.where(height == 95, SPAN, row + 2),
    )


def slab_of(start, half, frame, frames, conv_in):
    at = frame * COLS
    size = frames * COLS
    blocks = []
    for r in range(HALF):
        picks = tap_rows(start, half, r)
        blocks.append(
            jnp.concatenate([conv_in[row, at : at + size, :] for row in picks], axis=1)
        )
    return jnp.concatenate(blocks, axis=0)


def add_columns(half, frame, frames, low, left, total, first_out):
    size = frames * COLS
    for piece in range(total.shape[1] // LANES):
        column = left + piece * LANES
        tap = low + column // C
        at = (frame - tap) * COLS
        lane = column % C
        for r in range(HALF):
            part = total[r * size : (r + 1) * size, piece * LANES : (piece + 1) * LANES]
            first_out[half * HALF + r + 1, at : at + size, lane : lane + LANES] += part


NEW_FRAMES = ((2, 2, 0, 3), (4, 1, 1, 3), (5, 1, 2, 3))
OLD_FRAMES = ((1, 1, 0, 2), (0, 1, 0, 1))


def products(start, half, groups_of, w_mid, first_out, conv_in, between=None):
    pending = list(between or ())
    tiles = sum(-(-(high - low) * C // 256) for _, _, low, high in groups_of)
    done = 0
    count = len(pending)
    for frame, frames, low, high in groups_of:
        slab = slab_of(start, half, frame, frames, conv_in)
        width = (high - low) * C
        for left in range(0, width, 256):
            right = min(left + 256, width)
            total = jnp.dot(
                slab,
                w_mid[:, low * C + left : low * C + right],
                preferred_element_type=jnp.float32,
            )
            add_columns(half, frame, frames, low, left, total, first_out)
            done += 1
            while pending and (count - len(pending)) < count * done // tiles:
                pending.pop(0)()


def second_new(start, gain, w_mid, first_out, conv_a, conv_b):
    position = lax.broadcasted_iota(jnp.int32, (ROW, C), 0) & (COLS - 1)
    half_gain = 0.5 * gain[...].reshape(1, C)

    def rest(i):
        conv_b[i, CT * COLS :] = act_row(HALF + i, half_gain, first_out, position)

    later = [lambda i=i: rest(i) for i in range(2, SPAN)]
    products(start, 0, NEW_FRAMES, w_mid, first_out, conv_a, later)
    products(start, 1, NEW_FRAMES, w_mid, first_out, conv_b)


def second_old(start, live, w_mid, first_out, conv_a, conv_b, out):
    for half, conv in enumerate((conv_a, conv_b)):
        products(start, half, OLD_FRAMES, w_mid, first_out, conv)

    def emit(r, carry):
        out[r] = jnp.where(r < live, first_out[r + 1], 0.0).astype(jnp.bfloat16)
        return carry

    lax.fori_loop(0, BAND, emit, 0)


def block(
    clip_group,
    band_rows,
    new_lat,
    old_lat,
    old_act,
    gain,
    w_in,
    w_mid,
    out,
    raw_new,
    raw_old,
    raw_act,
    rows_lat,
    rows_act,
    pick,
    pairs,
    got_lat,
    got_act,
    clip_lat,
    clip_act,
    stack_lat,
    stack_act,
    slot_lat,
    slot_act,
    w_first,
    w_second,
    spread,
    taps,
    first_out,
    conv_a,
    conv_b,
    send_one,
    recv_one,
    send_two,
    recv_two,
    load,
):
    groups = lax.axis_size("seq")
    owners = lax.axis_size("dec")
    seq_at = lax.axis_index("seq")
    dec_at = lax.axis_index("dec")
    per_owner = new_lat.shape[0]

    raw = [
        pltpu.make_async_copy(new_lat, raw_new, load.at[12]),
        pltpu.make_async_copy(old_lat, raw_old, load.at[13]),
        pltpu.make_async_copy(old_act, raw_act, load.at[14]),
    ]
    loads = [
        pltpu.make_async_copy(
            w_mid.at[tap], w_second.at[:, tap * C : (tap + 1) * C], load.at[9 + tap]
        )
        for tap in range(3)
    ]
    for time_tap in range(3):
        for row_tap in range(3):
            tap = time_tap * 3 + row_tap
            at = row_tap * 256 + time_tap * 64
            loads.append(
                pltpu.make_async_copy(
                    w_in.at[tap], w_first.at[at : at + 3 * ZC, :], load.at[tap]
                )
            )
    for copy in raw + loads[:3]:
        copy.start()

    barrier = pltpu.get_barrier_semaphore()
    for step in range(1, groups):
        pl.semaphore_signal(
            barrier,
            inc=1,
            device_id=(lax.rem(seq_at + step, groups), dec_at),
            device_id_type=MESH,
        )

    def greet(step, carry):
        pl.semaphore_signal(
            barrier,
            inc=1,
            device_id=(seq_at, lax.rem(dec_at + step, owners)),
            device_id_type=MESH,
        )
        return carry

    lax.fori_loop(1, owners, greet, 0)

    for copy in raw[:2]:
        copy.wait()
    wide = COLS * ZC
    flat_lat = rows_lat.reshape(per_owner, wide // LANES, groups * PAD_FRAMES, LANES)
    flat_act = rows_act.reshape(per_owner, C // LANES, groups * CT * COLS, LANES)
    for t in range(per_owner):
        old = raw_old[t].astype(jnp.float32)
        new = raw_new[t].astype(jnp.float32)
        for frame in range(PAD_FRAMES):
            at = pl.ds(frame, groups, stride=PAD_FRAMES)
            for k in range(wide // LANES):
                lane = frame * wide + k * LANES
                if frame < CT:
                    values = old[:, lane : lane + LANES]
                elif frame < FRAMES:
                    lane -= CT * wide
                    values = new[:, lane : lane + LANES]
                else:
                    values = jnp.zeros((groups, LANES), jnp.float32)
                flat_lat[t, k, at, :] = values

    clips = []
    for group in range(groups):
        clip = jnp.int32(0)
        for i in range(groups):
            clip = clip + jnp.where(clip_group[seq_at, i] == group, i, 0)
        clips.append(jnp.minimum(clip, groups - 1))

    def by_group(rows, target, stack):
        for group in range(groups):
            for t in range(per_owner):
                parts = [rows[t, k, clips[group]] for k in range(rows.shape[1])]
                target[group, t] = jnp.concatenate(parts, axis=1).astype(jnp.bfloat16)
        stack[seq_at] = target[seq_at]

    by_group(rows_lat, clip_lat, stack_lat)
    pl.semaphore_wait(barrier, groups - 1 + owners - 1)

    def to_group(step, which):
        group = lax.rem(seq_at + step, groups)
        source, target = ((clip_lat, stack_lat), (clip_act, stack_act))[which]
        return pltpu.make_async_remote_copy(
            src_ref=source.at[group],
            dst_ref=target.at[seq_at],
            send_sem=send_one.at[which, step],
            recv_sem=recv_one.at[which, step],
            device_id=(group, dec_at),
            device_id_type=MESH,
        )

    for step in range(1, groups):
        to_group(step, 0).start()

    raw[2].wait()
    for t in range(per_owner):
        for q in range(CT * COLS):
            at = pl.ds(q, groups, stride=CT * COLS)
            for k in range(C // LANES):
                lane = q * C + k * LANES
                values = raw_act[t, :, lane : lane + LANES].astype(jnp.float32)
                flat_act[t, k, at, :] = values
    by_group(rows_act, clip_act, stack_act)
    for step in range(1, groups):
        to_group(step, 1).start()

    w_first[...] = jnp.zeros_like(w_first)
    for copy in loads[3:]:
        copy.start()
    make_pick(pick)


    def held_row(owner, start):
        first = lax.shift_right_arithmetic(start - 2 - dec_at + owners - 1, 5)
        return jnp.clip(first, 0, groups * per_owner - 1)

    def to_owner(step, which):
        owner = lax.rem(dec_at + step, owners)
        source, target = ((slot_lat, got_lat), (slot_act, got_act))[which]
        return pltpu.make_async_remote_copy(
            src_ref=source.at[owner],
            dst_ref=target.at[dec_at],
            send_sem=send_two.at[which, step],
            recv_sem=recv_two.at[which, step],
            device_id=(seq_at, owner),
            device_id_type=MESH,
        )

    def fill(which):
        stack, slot, got = (
            (stack_lat, slot_lat, got_lat),
            (stack_act, slot_act, got_act),
        )[which]
        for step in range(1, groups):
            to_group(step, which).wait_recv()

        def one(owner, start):
            row = held_row(owner, start)
            slot[owner] = stack[row // per_owner, lax.rem(row, per_owner)]
            return start + band_rows[seq_at, owner]

        lax.fori_loop(0, owners, one, jnp.int32(0))
        got[dec_at] = slot[dec_at]

    def pass_on(which):
        def launch(step, carry):
            to_owner(step, which).start()
            return carry

        lax.fori_loop(1, owners, launch, 0)

    def collect(which):
        def arrive(step, carry):
            to_owner(step, which).wait_recv()
            return carry

        lax.fori_loop(1, owners, arrive, 0)

    start = band_start(band_rows, seq_at, dec_at, owners)
    live = band_rows[seq_at, dec_at]
    fill(0)
    pass_on(0)
    fill(1)
    collect(0)
    pass_on(1)
    for copy in loads[3:]:
        copy.wait()
    first_stage(start, got_lat, pick, pairs, spread, taps, w_first, first_out)
    act_first(gain, first_out, conv_a, conv_b)
    for copy in loads[:3]:
        copy.wait()
    second_new(start, gain, w_second, first_out, conv_a, conv_b)
    collect(1)
    cache_stage(start, got_act, conv_a, conv_b)
    second_old(start, live, w_second, first_out, conv_a, conv_b, out)

    for which in range(2):
        for step in range(1, groups):
            to_group(step, which).wait_send()

        def finish(step, carry, which=which):
            to_owner(step, which).wait_send()
            return carry

        lax.fori_loop(1, owners, finish, 0)


def run_block(clip_group, band_rows, new_lat, old_lat, old_act, gain, w_in, w_mid):
    groups = lax.axis_size("seq")
    owners = lax.axis_size("dec")
    per_owner = new_lat.shape[0]
    lat_row, act_row = (PAD_FRAMES, COLS * ZC), (CT * COLS, C)
    bf16 = jnp.bfloat16
    vm = pl.BlockSpec(memory_space=pltpu.VMEM)
    sm = pl.BlockSpec(memory_space=pltpu.SMEM)
    hbm = pl.BlockSpec(memory_space=pl.ANY)
    return pl.pallas_call(
        block,
        out_shape=jax.ShapeDtypeStruct((BAND, ROW, C), bf16),
        in_specs=[sm, sm, hbm, hbm, hbm, vm, hbm, hbm],
        out_specs=vm,
        scratch_shapes=[
            pltpu.VMEM(new_lat.shape, bf16),
            pltpu.VMEM(old_lat.shape, bf16),
            pltpu.VMEM(old_act.shape, bf16),
            pltpu.VMEM((per_owner, COLS * ZC // LANES, groups, PAD_FRAMES, LANES), jnp.float32),
            pltpu.VMEM((per_owner, C // LANES, groups, CT * COLS, LANES), jnp.float32),
            pltpu.VMEM((COLS // TOGETHER, 2 * COLS * ZC, TOGETHER * LANES), bf16),
            pltpu.VMEM((EXT // 2, 2 * PAD_FRAMES, 2 * COLS * ZC), bf16),
            pltpu.VMEM((owners,) + lat_row, bf16),
            pltpu.VMEM((owners,) + act_row, bf16),
            pltpu.VMEM((groups, per_owner) + lat_row, bf16),
            pltpu.VMEM((groups, per_owner) + act_row, bf16),
            pltpu.VMEM((groups, per_owner) + lat_row, bf16),
            pltpu.VMEM((groups, per_owner) + act_row, bf16),
            pltpu.VMEM((owners,) + lat_row, bf16),
            pltpu.VMEM((owners,) + act_row, bf16),
            pltpu.VMEM((768, C), bf16),
            pltpu.VMEM((9 * C, 3 * C), bf16),
            pltpu.VMEM((EXT * PAD_FRAMES * COLS, LANES), jnp.float32),
            pltpu.VMEM((EXT + 1, FRAMES * COLS, LANES), bf16),
            pltpu.VMEM((MID, ROW, C), jnp.float32),
            pltpu.VMEM((SPAN + 1, FRAMES * COLS, 3 * C), bf16),
            pltpu.VMEM((SPAN + 1, FRAMES * COLS, 3 * C), bf16),
            pltpu.SemaphoreType.DMA((2, groups)),
            pltpu.SemaphoreType.DMA((2, groups)),
            pltpu.SemaphoreType.DMA((2, owners)),
            pltpu.SemaphoreType.DMA((2, owners)),
            pltpu.SemaphoreType.DMA((15,)),
        ],
        compiler_params=pltpu.CompilerParams(
            collective_id=0, has_side_effects=True, vmem_limit_bytes=56 << 20
        ),
        name="block",
    )(clip_group, band_rows, new_lat, old_lat, old_act, gain, w_in, w_mid)


def shards(latents, cache_lat, cache_act, w_in, w_mid, norm_gain, clip_group, band_rows):
    def by_time(rows):
        return jnp.transpose(rows[0, :, :, 0, :], (1, 0, 2))

    out = run_block(
        clip_group,
        band_rows,
        by_time(latents),
        by_time(cache_lat),
        by_time(cache_act),
        norm_gain,
        w_in.reshape(9, 3 * ZC, C),
        w_mid.reshape(3, 9 * C, C),
    )
    return out.reshape(1, 1, BAND, F, COLS, C)


def solution(mesh):
    placed = P("seq", None, None, "dec", None)
    return jax.shard_map(
        shards,
        mesh=mesh,
        in_specs=(placed, placed, placed, P(), P(), P(), P(), P()),
        out_specs=P("seq", "dec", None, None, None, None),
        check_vma=False,
    )
```

```python
import jax
import jax.numpy as jnp
from jax import lax
from jax.experimental import pallas as pl
from jax.experimental.pallas import tpu as pltpu
from jax.sharding import PartitionSpec as P

F = 4
CT = 2
COLS = 16
ZC = 16
C = 384
FRAMES = F + CT
PAD_FRAMES = 8
ROW = F * COLS
BAND = 24
EXT = BAND + 4
MID = BAND + 2
LANES = 128
TOGETHER = 4
EPSILON = 1e-06
MESH = pl.DeviceIdType.MESH


def band_start(band_rows, group, owner, owners):
    return lax.fori_loop(
        0,
        owners,
        lambda o, total: total + jnp.where(o < owner, band_rows[group, o], 0),
        jnp.int32(0),
    )


def make_pick(pick):
    shape = (2 * COLS * ZC, LANES)
    source = lax.broadcasted_iota(jnp.int32, shape, 0)
    lane = lax.broadcasted_iota(jnp.int32, shape, 1)
    frame = source >= COLS * ZC
    inner = jnp.where(frame, lane - 64, lane)
    here = source & (COLS * ZC - 1)

    inside = (inner >= 0) & (inner < 3 * ZC)

    def some(part, carry):
        for i in range(TOGETHER):
            wanted = here - ZC * (part * TOGETHER + i - 1)
            block = jnp.where(inside & (inner == wanted), 1.0, 0.0).astype(jnp.bfloat16)
            pick[part, :, i * LANES : (i + 1) * LANES] = block
        return carry

    lax.fori_loop(0, COLS // TOGETHER, some, 0)


def first_stage(start, got_lat, pick, pairs, spread, taps, w_first, first_out):
    def gather(i, carry):
        rows = []
        for k in range(2):
            frames = got_lat[(start - 2 + 2 * i + k) & 31].astype(jnp.float32)
            after = pltpu.roll(frames, PAD_FRAMES - 1, 0)
            rows.append(jnp.concatenate([frames, after], axis=1))
        pairs[i] = jnp.concatenate(rows, axis=0).astype(jnp.bfloat16)
        return carry

    lax.fori_loop(0, EXT // 2, gather, 0)
    source = pairs[...].reshape(EXT * PAD_FRAMES, 2 * COLS * ZC)

    def columns(part, carry):
        block = jnp.dot(source, pick[part], preferred_element_type=jnp.float32)
        for i in range(TOGETHER):
            col = part * TOGETHER + i
            rows = pl.ds(col, EXT * PAD_FRAMES, stride=COLS)
            spread[rows, :] = block[:, i * LANES : (i + 1) * LANES]
        return carry

    lax.fori_loop(0, COLS // TOGETHER, columns, 0)
    taps[EXT] = jnp.zeros((FRAMES * COLS, LANES), jnp.bfloat16)

    def narrow(j, carry):
        at = pl.multiple_of(j * PAD_FRAMES * COLS, PAD_FRAMES * COLS)
        taps[j] = spread[pl.ds(at, FRAMES * COLS), :].astype(jnp.bfloat16)
        return carry

    lax.fori_loop(0, EXT, narrow, 0)

    rows = MID // 2
    for part in range(2):
        blocks = []
        for r in range(rows):
            j = part * rows + r + 1
            height = lax.rem(start - 2 + j + 96, 96)
            picks = (
                jnp.where(height == 0, EXT, j - 1),
                j,
                jnp.where(height == 95, EXT, j + 1),
            )
            pieces = []
            for at in picks:
                block = taps[at]
                pieces += [block[:ROW], block[2 * COLS : 2 * COLS + ROW]]
            blocks.append(jnp.concatenate(pieces, axis=1))
        slab = jnp.concatenate(blocks, axis=0)
        total = jnp.dot(slab, w_first[...], preferred_element_type=jnp.float32)
        first_out[part * rows : (part + 1) * rows] = total.reshape(rows, ROW, C)


def shifted(values, position):
    count = values.shape[0]
    before = jnp.where(position == 0, 0.0, pltpu.roll(values, 1, 0))
    after = jnp.where(position == COLS - 1, 0.0, pltpu.roll(values, count - 1, 0))
    return jnp.concatenate([before, values, after], axis=1).astype(jnp.bfloat16)


HALF = BAND // 2
SPAN = HALF + 2


def act_row(row, gain, first_out, position):
    values = first_out[row]
    mean = jnp.mean(values * values, axis=1, keepdims=True)
    half = values * lax.rsqrt(mean + EPSILON) * gain
    return shifted(half + half * jnp.tanh(half), position)


def act_first(gain, first_out, conv_a, conv_b):
    position = lax.broadcasted_iota(jnp.int32, (ROW, C), 0) & (COLS - 1)
    half_gain = 0.5 * gain[...].reshape(1, C)
    zero = jnp.zeros((FRAMES * COLS, 3 * C), jnp.bfloat16)
    conv_a[SPAN] = zero
    conv_b[SPAN] = zero

    def one(i, carry):
        conv_a[i, CT * COLS :] = act_row(i, half_gain, first_out, position)
        return carry

    lax.fori_loop(0, SPAN, one, 0)
    for i in range(2):
        conv_b[i, CT * COLS :] = conv_a[HALF + i, CT * COLS :]


def cache_stage(start, got_act, conv_a, conv_b):
    position = lax.broadcasted_iota(jnp.int32, (CT * COLS, C), 0) & (COLS - 1)

    def one(i, carry):
        for half, conv in enumerate((conv_a, conv_b)):
            at = start - 1 + i + half * HALF
            values = got_act[at & 31].astype(jnp.float32)
            conv[i, : CT * COLS] = shifted(values, position)
        return carry

    lax.fori_loop(0, SPAN, one, 0)


def tap_rows(start, half, row):
    height = lax.rem(start + half * HALF + row, 96)
    return (
        jnp.where(height == 0, SPAN, row),
        row + 1,
        jnp.where(height == 95, SPAN, row + 2),
    )


def slab_of(start, half, frame, frames, conv_in):
    at = frame * COLS
    size = frames * COLS
    blocks = []
    for r in range(HALF):
        picks = tap_rows(start, half, r)
        blocks.append(
            jnp.concatenate([conv_in[row, at : at + size, :] for row in picks], axis=1)
        )
    return jnp.concatenate(blocks, axis=0)


def add_columns(half, frame, frames, low, left, total, first_out):
    size = frames * COLS
    for piece in range(total.shape[1] // LANES):
        column = left + piece * LANES
        tap = low + column // C
        at = (frame - tap) * COLS
        lane = column % C
        for r in range(HALF):
            part = total[r * size : (r + 1) * size, piece * LANES : (piece + 1) * LANES]
            first_out[half * HALF + r + 1, at : at + size, lane : lane + LANES] += part


NEW_FRAMES = ((2, 2, 0, 3), (4, 1, 1, 3), (5, 1, 2, 3))
OLD_FRAMES = ((1, 1, 0, 2), (0, 1, 0, 1))


def products(start, half, groups_of, w_mid, first_out, conv_in, between=None):
    pending = list(between or ())
    tiles = sum(-(-(high - low) * C // 256) for _, _, low, high in groups_of)
    done = 0
    count = len(pending)
    for frame, frames, low, high in groups_of:
        slab = slab_of(start, half, frame, frames, conv_in)
        width = (high - low) * C
        for left in range(0, width, 256):
            right = min(left + 256, width)
            total = jnp.dot(
                slab,
                w_mid[:, low * C + left : low * C + right],
                preferred_element_type=jnp.float32,
            )
            add_columns(half, frame, frames, low, left, total, first_out)
            done += 1
            while pending and (count - len(pending)) < -(-count * done // tiles):
                pending.pop(0)()


def second_new(start, gain, w_mid, first_out, conv_a, conv_b):
    position = lax.broadcasted_iota(jnp.int32, (ROW, C), 0) & (COLS - 1)
    half_gain = 0.5 * gain[...].reshape(1, C)

    def rest(i):
        conv_b[i, CT * COLS :] = act_row(HALF + i, half_gain, first_out, position)

    later = [lambda i=i: rest(i) for i in range(2, SPAN)]
    products(start, 0, NEW_FRAMES, w_mid, first_out, conv_a, later)
    products(start, 1, NEW_FRAMES, w_mid, first_out, conv_b)


def second_old(start, live, w_mid, first_out, conv_a, conv_b, out, leave):
    def emit(r):
        out[r] = jnp.where(r < live, first_out[r + 1], 0.0).astype(jnp.bfloat16)

    def emit_half(half):
        for r in range(half * HALF, (half + 1) * HALF):
            emit(r)
        leave(half)

    products(start, 0, OLD_FRAMES, w_mid, first_out, conv_a)
    products(start, 1, OLD_FRAMES, w_mid, first_out, conv_b, [lambda: emit_half(0)])
    emit_half(1)


def block(
    clip_group,
    band_rows,
    new_lat,
    old_lat,
    old_act,
    gain,
    w_in,
    w_mid,
    out,
    staged,
    raw_new,
    raw_old,
    raw_act,
    rows_lat,
    rows_act,
    pick,
    pairs,
    got_lat,
    got_act,
    clip_lat,
    clip_act,
    stack_lat,
    stack_act,
    slot_lat,
    slot_act,
    w_first,
    w_second,
    spread,
    taps,
    first_out,
    conv_a,
    conv_b,
    send_one,
    recv_one,
    send_two,
    recv_two,
    load,
):
    groups = lax.axis_size("seq")
    owners = lax.axis_size("dec")
    seq_at = lax.axis_index("seq")
    dec_at = lax.axis_index("dec")
    per_owner = new_lat.shape[0]

    raw = [
        pltpu.make_async_copy(new_lat, raw_new, load.at[12]),
        pltpu.make_async_copy(old_lat, raw_old, load.at[13]),
        pltpu.make_async_copy(old_act, raw_act, load.at[14]),
    ]
    loads = [
        pltpu.make_async_copy(
            w_mid.at[tap], w_second.at[:, tap * C : (tap + 1) * C], load.at[9 + tap]
        )
        for tap in range(3)
    ]
    for time_tap in range(3):
        for row_tap in range(3):
            tap = time_tap * 3 + row_tap
            at = row_tap * 256 + time_tap * 64
            loads.append(
                pltpu.make_async_copy(
                    w_in.at[tap], w_first.at[at : at + 3 * ZC, :], load.at[tap]
                )
            )
    for copy in raw + loads[:3]:
        copy.start()

    barrier = pltpu.get_barrier_semaphore()
    for step in range(1, groups):
        pl.semaphore_signal(
            barrier,
            inc=1,
            device_id=(lax.rem(seq_at + step, groups), dec_at),
            device_id_type=MESH,
        )

    def greet(step, carry):
        pl.semaphore_signal(
            barrier,
            inc=1,
            device_id=(seq_at, lax.rem(dec_at + step, owners)),
            device_id_type=MESH,
        )
        return carry

    lax.fori_loop(1, owners, greet, 0)

    for copy in raw[:2]:
        copy.wait()
    wide = COLS * ZC
    flat_lat = rows_lat.reshape(per_owner, wide // LANES, groups * PAD_FRAMES, LANES)
    flat_act = rows_act.reshape(per_owner, C // LANES, groups * CT * COLS, LANES)
    for t in range(per_owner):
        old = raw_old[t].astype(jnp.float32)
        new = raw_new[t].astype(jnp.float32)
        for frame in range(PAD_FRAMES):
            at = pl.ds(frame, groups, stride=PAD_FRAMES)
            for k in range(wide // LANES):
                lane = frame * wide + k * LANES
                if frame < CT:
                    values = old[:, lane : lane + LANES]
                elif frame < FRAMES:
                    lane -= CT * wide
                    values = new[:, lane : lane + LANES]
                else:
                    values = jnp.zeros((groups, LANES), jnp.float32)
                flat_lat[t, k, at, :] = values

    clips = []
    for group in range(groups):
        clip = jnp.int32(0)
        for i in range(groups):
            clip = clip + jnp.where(clip_group[seq_at, i] == group, i, 0)
        clips.append(jnp.minimum(clip, groups - 1))

    def by_group(rows, target, stack):
        for group in range(groups):
            for t in range(per_owner):
                parts = [rows[t, k, clips[group]] for k in range(rows.shape[1])]
                target[group, t] = jnp.concatenate(parts, axis=1).astype(jnp.bfloat16)
        stack[seq_at] = target[seq_at]

    by_group(rows_lat, clip_lat, stack_lat)
    pl.semaphore_wait(barrier, groups - 1 + owners - 1)

    def to_group(step, which):
        group = lax.rem(seq_at + step, groups)
        source, target = ((clip_lat, stack_lat), (clip_act, stack_act))[which]
        return pltpu.make_async_remote_copy(
            src_ref=source.at[group],
            dst_ref=target.at[seq_at],
            send_sem=send_one.at[which, step],
            recv_sem=recv_one.at[which, step],
            device_id=(group, dec_at),
            device_id_type=MESH,
        )

    for step in range(1, groups):
        to_group(step, 0).start()

    raw[2].wait()
    for t in range(per_owner):
        for q in range(CT * COLS):
            at = pl.ds(q, groups, stride=CT * COLS)
            for k in range(C // LANES):
                lane = q * C + k * LANES
                values = raw_act[t, :, lane : lane + LANES].astype(jnp.float32)
                flat_act[t, k, at, :] = values
    by_group(rows_act, clip_act, stack_act)
    for step in range(1, groups):
        to_group(step, 1).start()

    w_first[...] = jnp.zeros_like(w_first)
    for copy in loads[3:]:
        copy.start()
    make_pick(pick)


    def held_row(owner, start):
        first = lax.shift_right_arithmetic(start - 2 - dec_at + owners - 1, 5)
        return jnp.clip(first, 0, groups * per_owner - 1)

    def to_owner(step, which):
        owner = lax.rem(dec_at + step, owners)
        source, target = ((slot_lat, got_lat), (slot_act, got_act))[which]
        return pltpu.make_async_remote_copy(
            src_ref=source.at[owner],
            dst_ref=target.at[dec_at],
            send_sem=send_two.at[which],
            recv_sem=recv_two.at[which],
            device_id=(seq_at, owner),
            device_id_type=MESH,
        )

    def fill(which):
        stack, slot, got = (
            (stack_lat, slot_lat, got_lat),
            (stack_act, slot_act, got_act),
        )[which]
        for step in range(1, groups):
            to_group(step, which).wait_recv()

        def one(owner, start):
            row = held_row(owner, start)
            slot[owner] = stack[row // per_owner, lax.rem(row, per_owner)]
            return start + band_rows[seq_at, owner]

        lax.fori_loop(0, owners, one, jnp.int32(0))
        got[dec_at] = slot[dec_at]

    def pass_on(which):
        def launch(step, carry):
            to_owner(step, which).start()
            return carry

        lax.fori_loop(1, owners, launch, 0)

    def all_owners(which):
        source, target = ((slot_lat, got_lat), (slot_act, got_act))[which]
        rows = pl.ds(0, owners - 1)
        return pltpu.make_async_remote_copy(
            src_ref=source.at[rows],
            dst_ref=target.at[rows],
            send_sem=send_two.at[which],
            recv_sem=recv_two.at[which],
            device_id=(seq_at, lax.rem(dec_at + 1, owners)),
            device_id_type=MESH,
        )

    start = band_start(band_rows, seq_at, dec_at, owners)
    live = band_rows[seq_at, dec_at]
    fill(0)
    pass_on(0)
    fill(1)
    all_owners(0).wait_recv()
    pass_on(1)
    for copy in loads[3:]:
        copy.wait()
    first_stage(start, got_lat, pick, pairs, spread, taps, w_first, first_out)
    act_first(gain, first_out, conv_a, conv_b)
    for copy in loads[:3]:
        copy.wait()
    second_new(start, gain, w_second, first_out, conv_a, conv_b)
    all_owners(1).wait_recv()
    cache_stage(start, got_act, conv_a, conv_b)

    def leaving(half):
        rows = pl.ds(half * HALF, HALF)
        return pltpu.make_async_copy(staged.at[rows], out.at[rows], load.at[15 + half])

    second_old(
        start,
        live,
        w_second,
        first_out,
        conv_a,
        conv_b,
        staged,
        lambda half: leaving(half).start(),
    )

    for which in range(2):
        for step in range(1, groups):
            to_group(step, which).wait_send()
        all_owners(which).wait_send()
    for half in range(2):
        leaving(half).wait()


def run_block(clip_group, band_rows, new_lat, old_lat, old_act, gain, w_in, w_mid):
    groups = lax.axis_size("seq")
    owners = lax.axis_size("dec")
    per_owner = new_lat.shape[0]
    lat_row, act_row = (PAD_FRAMES, COLS * ZC), (CT * COLS, C)
    bf16 = jnp.bfloat16
    vm = pl.BlockSpec(memory_space=pltpu.VMEM)
    sm = pl.BlockSpec(memory_space=pltpu.SMEM)
    hbm = pl.BlockSpec(memory_space=pl.ANY)
    return pl.pallas_call(
        block,
        out_shape=jax.ShapeDtypeStruct((BAND, ROW, C), bf16),
        in_specs=[sm, sm, hbm, hbm, hbm, vm, hbm, hbm],
        out_specs=hbm,
        scratch_shapes=[
            pltpu.VMEM((BAND, ROW, C), bf16),
            pltpu.VMEM(new_lat.shape, bf16),
            pltpu.VMEM(old_lat.shape, bf16),
            pltpu.VMEM(old_act.shape, bf16),
            pltpu.VMEM((per_owner, COLS * ZC // LANES, groups, PAD_FRAMES, LANES), jnp.float32),
            pltpu.VMEM((per_owner, C // LANES, groups, CT * COLS, LANES), jnp.float32),
            pltpu.VMEM((COLS // TOGETHER, 2 * COLS * ZC, TOGETHER * LANES), bf16),
            pltpu.VMEM((EXT // 2, 2 * PAD_FRAMES, 2 * COLS * ZC), bf16),
            pltpu.VMEM((owners,) + lat_row, bf16),
            pltpu.VMEM((owners,) + act_row, bf16),
            pltpu.VMEM((groups, per_owner) + lat_row, bf16),
            pltpu.VMEM((groups, per_owner) + act_row, bf16),
            pltpu.VMEM((groups, per_owner) + lat_row, bf16),
            pltpu.VMEM((groups, per_owner) + act_row, bf16),
            pltpu.VMEM((owners,) + lat_row, bf16),
            pltpu.VMEM((owners,) + act_row, bf16),
            pltpu.VMEM((768, C), bf16),
            pltpu.VMEM((9 * C, 3 * C), bf16),
            pltpu.VMEM((EXT * PAD_FRAMES * COLS, LANES), jnp.float32),
            pltpu.VMEM((EXT + 1, FRAMES * COLS, LANES), bf16),
            pltpu.VMEM((MID, ROW, C), jnp.float32),
            pltpu.VMEM((SPAN + 1, FRAMES * COLS, 3 * C), bf16),
            pltpu.VMEM((SPAN + 1, FRAMES * COLS, 3 * C), bf16),
            pltpu.SemaphoreType.DMA((2, groups)),
            pltpu.SemaphoreType.DMA((2, groups)),
            pltpu.SemaphoreType.DMA((2,)),
            pltpu.SemaphoreType.DMA((2,)),
            pltpu.SemaphoreType.DMA((17,)),
        ],
        compiler_params=pltpu.CompilerParams(
            collective_id=0, has_side_effects=True, vmem_limit_bytes=56 << 20
        ),
        name="block",
    )(clip_group, band_rows, new_lat, old_lat, old_act, gain, w_in, w_mid)


def shards(latents, cache_lat, cache_act, w_in, w_mid, norm_gain, clip_group, band_rows):
    def by_time(rows):
        return jnp.transpose(rows[0, :, :, 0, :], (1, 0, 2))

    out = run_block(
        clip_group,
        band_rows,
        by_time(latents),
        by_time(cache_lat),
        by_time(cache_act),
        norm_gain,
        w_in.reshape(9, 3 * ZC, C),
        w_mid.reshape(3, 9 * C, C),
    )
    return out.reshape(1, 1, BAND, F, COLS, C)


def solution(mesh):
    placed = P("seq", None, None, "dec", None)
    return jax.shard_map(
        shards,
        mesh=mesh,
        in_specs=(placed, placed, placed, P(), P(), P(), P(), P()),
        out_specs=P("seq", "dec", None, None, None, None),
        check_vma=False,
    )
```

```python
import jax
import jax.numpy as jnp
from jax import lax
from jax.experimental import pallas as pl
from jax.experimental.pallas import tpu as pltpu
from jax.sharding import PartitionSpec as P

F = 4
CT = 2
COLS = 16
ZC = 16
C = 384
FRAMES = F + CT
PAD_FRAMES = 8
ROW = F * COLS
BAND = 24
EXT = BAND + 4
MID = BAND + 2
LANES = 128
TOGETHER = 4
EPSILON = 1e-06
MESH = pl.DeviceIdType.MESH


def band_start(band_rows, group, owner, owners):
    return lax.fori_loop(
        0,
        owners,
        lambda o, total: total + jnp.where(o < owner, band_rows[group, o], 0),
        jnp.int32(0),
    )


def make_pick(pick):
    shape = (2 * COLS * ZC, LANES)
    source = lax.broadcasted_iota(jnp.int32, shape, 0)
    lane = lax.broadcasted_iota(jnp.int32, shape, 1)
    frame = source >= COLS * ZC
    inner = jnp.where(frame, lane - 64, lane)
    here = source & (COLS * ZC - 1)

    inside = (inner >= 0) & (inner < 3 * ZC)

    def some(part, carry):
        for i in range(TOGETHER):
            wanted = here - ZC * (part * TOGETHER + i - 1)
            block = jnp.where(inside & (inner == wanted), 1.0, 0.0).astype(jnp.bfloat16)
            pick[part, :, i * LANES : (i + 1) * LANES] = block
        return carry

    lax.fori_loop(0, COLS // TOGETHER, some, 0)


def first_stage(start, got_lat, pick, pairs, spread, taps, w_first, first_out):
    def gather(i, carry):
        rows = []
        for k in range(2):
            frames = got_lat[(start - 2 + 2 * i + k) & 31].astype(jnp.float32)
            after = pltpu.roll(frames, PAD_FRAMES - 1, 0)
            rows.append(jnp.concatenate([frames, after], axis=1))
        pairs[i] = jnp.concatenate(rows, axis=0).astype(jnp.bfloat16)
        return carry

    lax.fori_loop(0, EXT // 2, gather, 0, unroll=7)
    source = pairs[...].reshape(EXT * PAD_FRAMES, 2 * COLS * ZC)

    def columns(part, carry):
        block = jnp.dot(source, pick[part], preferred_element_type=jnp.float32)
        for i in range(TOGETHER):
            col = part * TOGETHER + i
            rows = pl.ds(col, EXT * PAD_FRAMES, stride=COLS)
            spread[rows, :] = block[:, i * LANES : (i + 1) * LANES]
        return carry

    lax.fori_loop(0, COLS // TOGETHER, columns, 0, unroll=True)
    taps[EXT] = jnp.zeros((FRAMES * COLS, LANES), jnp.bfloat16)

    def narrow(j, carry):
        at = pl.multiple_of(j * PAD_FRAMES * COLS, PAD_FRAMES * COLS)
        taps[j] = spread[pl.ds(at, FRAMES * COLS), :].astype(jnp.bfloat16)
        return carry

    lax.fori_loop(0, EXT, narrow, 0, unroll=7)

    rows = MID // 2
    for part in range(2):
        blocks = []
        for r in range(rows):
            j = part * rows + r + 1
            height = lax.rem(start - 2 + j + 96, 96)
            picks = (
                jnp.where(height == 0, EXT, j - 1),
                j,
                jnp.where(height == 95, EXT, j + 1),
            )
            pieces = []
            for at in picks:
                block = taps[at]
                pieces += [block[:ROW], block[2 * COLS : 2 * COLS + ROW]]
            blocks.append(jnp.concatenate(pieces, axis=1))
        slab = jnp.concatenate(blocks, axis=0)
        total = jnp.dot(slab, w_first[...], preferred_element_type=jnp.float32)
        first_out[part * rows : (part + 1) * rows] = total.reshape(rows, ROW, C)


def shifted(values, position):
    count = values.shape[0]
    before = jnp.where(position == 0, 0.0, pltpu.roll(values, 1, 0))
    after = jnp.where(position == COLS - 1, 0.0, pltpu.roll(values, count - 1, 0))
    return jnp.concatenate([before, values, after], axis=1).astype(jnp.bfloat16)


HALF = BAND // 2
SPAN = HALF + 2


def act_row(row, gain, first_out, position):
    values = first_out[row]
    mean = jnp.mean(values * values, axis=1, keepdims=True)
    half = values * lax.rsqrt(mean + EPSILON) * gain
    return shifted(half + half * jnp.tanh(half), position)


def act_first(gain, first_out, conv_a, conv_b):
    position = lax.broadcasted_iota(jnp.int32, (ROW, C), 0) & (COLS - 1)
    half_gain = 0.5 * gain[...].reshape(1, C)
    zero = jnp.zeros((FRAMES * COLS, 3 * C), jnp.bfloat16)
    conv_a[SPAN] = zero
    conv_b[SPAN] = zero

    def one(i, carry):
        conv_a[i, CT * COLS :] = act_row(i, half_gain, first_out, position)
        return carry

    lax.fori_loop(0, SPAN, one, 0, unroll=7)
    for i in range(2):
        conv_b[i, CT * COLS :] = conv_a[HALF + i, CT * COLS :]


def cache_stage(start, got_act, conv_a, conv_b):
    position = lax.broadcasted_iota(jnp.int32, (CT * COLS, C), 0) & (COLS - 1)

    def one(i, carry):
        for half, conv in enumerate((conv_a, conv_b)):
            at = start - 1 + i + half * HALF
            values = got_act[at & 31].astype(jnp.float32)
            conv[i, : CT * COLS] = shifted(values, position)
        return carry

    lax.fori_loop(0, SPAN, one, 0, unroll=7)


def tap_rows(start, half, row):
    height = lax.rem(start + half * HALF + row, 96)
    return (
        jnp.where(height == 0, SPAN, row),
        row + 1,
        jnp.where(height == 95, SPAN, row + 2),
    )


def slab_of(start, half, frame, frames, conv_in):
    at = frame * COLS
    size = frames * COLS
    blocks = []
    for r in range(HALF):
        picks = tap_rows(start, half, r)
        blocks.append(
            jnp.concatenate([conv_in[row, at : at + size, :] for row in picks], axis=1)
        )
    return jnp.concatenate(blocks, axis=0)


def add_columns(half, frame, frames, low, left, total, first_out):
    size = frames * COLS
    for piece in range(total.shape[1] // LANES):
        column = left + piece * LANES
        tap = low + column // C
        at = (frame - tap) * COLS
        lane = column % C
        for r in range(HALF):
            part = total[r * size : (r + 1) * size, piece * LANES : (piece + 1) * LANES]
            first_out[half * HALF + r + 1, at : at + size, lane : lane + LANES] += part


NEW_FRAMES = ((2, 2, 0, 3), (4, 1, 1, 3), (5, 1, 2, 3))
OLD_FRAMES = ((1, 1, 0, 2), (0, 1, 0, 1))


def products(start, half, groups_of, w_mid, first_out, conv_in, between=None):
    pending = list(between or ())
    tiles = sum(-(-(high - low) * C // 256) for _, _, low, high in groups_of)
    done = 0
    count = len(pending)
    for frame, frames, low, high in groups_of:
        slab = slab_of(start, half, frame, frames, conv_in)
        width = (high - low) * C
        for left in range(0, width, 256):
            right = min(left + 256, width)
            total = jnp.dot(
                slab,
                w_mid[:, low * C + left : low * C + right],
                preferred_element_type=jnp.float32,
            )
            add_columns(half, frame, frames, low, left, total, first_out)
            done += 1
            while pending and (count - len(pending)) < -(-count * done // tiles):
                pending.pop(0)()


def second_new(start, gain, w_mid, first_out, conv_a, conv_b):
    position = lax.broadcasted_iota(jnp.int32, (ROW, C), 0) & (COLS - 1)
    half_gain = 0.5 * gain[...].reshape(1, C)

    def rest(i):
        conv_b[i, CT * COLS :] = act_row(HALF + i, half_gain, first_out, position)

    later = [lambda i=i: rest(i) for i in range(2, SPAN)]
    products(start, 0, NEW_FRAMES, w_mid, first_out, conv_a, later)
    products(start, 1, NEW_FRAMES, w_mid, first_out, conv_b)


def second_old(start, live, w_mid, first_out, conv_a, conv_b, out, leave):
    def emit(r):
        out[r] = jnp.where(r < live, first_out[r + 1], 0.0).astype(jnp.bfloat16)

    def emit_half(half):
        for r in range(half * HALF, (half + 1) * HALF):
            emit(r)
        leave(half)

    products(start, 0, OLD_FRAMES, w_mid, first_out, conv_a)
    products(start, 1, OLD_FRAMES, w_mid, first_out, conv_b, [lambda: emit_half(0)])
    emit_half(1)


def block(
    clip_group,
    band_rows,
    new_lat,
    old_lat,
    old_act,
    gain,
    w_in,
    w_mid,
    out,
    staged,
    raw_new,
    raw_old,
    raw_act,
    rows_lat,
    rows_act,
    pick,
    pairs,
    got_lat,
    got_act,
    clip_lat,
    clip_act,
    stack_lat,
    stack_act,
    slot_lat,
    slot_act,
    w_first,
    w_second,
    spread,
    taps,
    first_out,
    conv_a,
    conv_b,
    send_one,
    recv_one,
    send_two,
    recv_two,
    load,
):
    groups = lax.axis_size("seq")
    owners = lax.axis_size("dec")
    seq_at = lax.axis_index("seq")
    dec_at = lax.axis_index("dec")
    per_owner = new_lat.shape[0]

    raw = [
        pltpu.make_async_copy(new_lat, raw_new, load.at[12]),
        pltpu.make_async_copy(old_lat, raw_old, load.at[13]),
        pltpu.make_async_copy(old_act, raw_act, load.at[14]),
    ]
    loads = [
        pltpu.make_async_copy(
            w_mid.at[tap], w_second.at[:, tap * C : (tap + 1) * C], load.at[9 + tap]
        )
        for tap in range(3)
    ]
    for time_tap in range(3):
        for row_tap in range(3):
            tap = time_tap * 3 + row_tap
            at = row_tap * 256 + time_tap * 64
            loads.append(
                pltpu.make_async_copy(
                    w_in.at[tap], w_first.at[at : at + 3 * ZC, :], load.at[tap]
                )
            )
    for copy in raw + loads[:3]:
        copy.start()

    barrier = pltpu.get_barrier_semaphore()
    for step in range(1, groups):
        pl.semaphore_signal(
            barrier,
            inc=1,
            device_id=(lax.rem(seq_at + step, groups), dec_at),
            device_id_type=MESH,
        )

    def greet(step, carry):
        pl.semaphore_signal(
            barrier,
            inc=1,
            device_id=(seq_at, lax.rem(dec_at + step, owners)),
            device_id_type=MESH,
        )
        return carry

    lax.fori_loop(1, owners, greet, 0)

    for copy in raw[:2]:
        copy.wait()
    wide = COLS * ZC
    flat_lat = rows_lat.reshape(per_owner, wide // LANES, groups * PAD_FRAMES, LANES)
    flat_act = rows_act.reshape(per_owner, C // LANES, groups * CT * COLS, LANES)
    for t in range(per_owner):
        old = raw_old[t].astype(jnp.float32)
        new = raw_new[t].astype(jnp.float32)
        for frame in range(PAD_FRAMES):
            at = pl.ds(frame, groups, stride=PAD_FRAMES)
            for k in range(wide // LANES):
                lane = frame * wide + k * LANES
                if frame < CT:
                    values = old[:, lane : lane + LANES]
                elif frame < FRAMES:
                    lane -= CT * wide
                    values = new[:, lane : lane + LANES]
                else:
                    values = jnp.zeros((groups, LANES), jnp.float32)
                flat_lat[t, k, at, :] = values

    clips = []
    for group in range(groups):
        clip = jnp.int32(0)
        for i in range(groups):
            clip = clip + jnp.where(clip_group[seq_at, i] == group, i, 0)
        clips.append(jnp.minimum(clip, groups - 1))

    def by_group(rows, target, stack):
        for group in range(groups):
            for t in range(per_owner):
                parts = [rows[t, k, clips[group]] for k in range(rows.shape[1])]
                target[group, t] = jnp.concatenate(parts, axis=1).astype(jnp.bfloat16)
        stack[seq_at] = target[seq_at]

    by_group(rows_lat, clip_lat, stack_lat)
    pl.semaphore_wait(barrier, groups - 1 + owners - 1)

    def to_group(step, which):
        group = lax.rem(seq_at + step, groups)
        source, target = ((clip_lat, stack_lat), (clip_act, stack_act))[which]
        return pltpu.make_async_remote_copy(
            src_ref=source.at[group],
            dst_ref=target.at[seq_at],
            send_sem=send_one.at[which, step],
            recv_sem=recv_one.at[which, step],
            device_id=(group, dec_at),
            device_id_type=MESH,
        )

    for step in range(1, groups):
        to_group(step, 0).start()

    raw[2].wait()
    for t in range(per_owner):
        for q in range(CT * COLS):
            at = pl.ds(q, groups, stride=CT * COLS)
            for k in range(C // LANES):
                lane = q * C + k * LANES
                values = raw_act[t, :, lane : lane + LANES].astype(jnp.float32)
                flat_act[t, k, at, :] = values
    by_group(rows_act, clip_act, stack_act)
    for step in range(1, groups):
        to_group(step, 1).start()

    w_first[...] = jnp.zeros_like(w_first)
    for copy in loads[3:]:
        copy.start()
    make_pick(pick)


    def held_row(owner, start):
        first = lax.shift_right_arithmetic(start - 2 - dec_at + owners - 1, 5)
        return jnp.clip(first, 0, groups * per_owner - 1)

    def to_owner(step, which):
        owner = lax.rem(dec_at + 1 + lax.rem(step + 9, owners - 1), owners)
        source, target = ((slot_lat, got_lat), (slot_act, got_act))[which]
        return pltpu.make_async_remote_copy(
            src_ref=source.at[owner],
            dst_ref=target.at[dec_at],
            send_sem=send_two.at[which],
            recv_sem=recv_two.at[which],
            device_id=(seq_at, owner),
            device_id_type=MESH,
        )

    def fill(which):
        stack, slot, got = (
            (stack_lat, slot_lat, got_lat),
            (stack_act, slot_act, got_act),
        )[which]
        for step in range(1, groups):
            to_group(step, which).wait_recv()

        def one(owner, start):
            row = held_row(owner, start)
            slot[owner] = stack[row // per_owner, lax.rem(row, per_owner)]
            return start + band_rows[seq_at, owner]

        lax.fori_loop(0, owners, one, jnp.int32(0), unroll=4)
        got[dec_at] = slot[dec_at]

    def pass_on(which):
        def launch(step, carry):
            to_owner(step, which).start()
            return carry

        lax.fori_loop(1, owners, launch, 0, unroll=True)

    def all_owners(which):
        source, target = ((slot_lat, got_lat), (slot_act, got_act))[which]
        rows = pl.ds(0, owners - 1)
        return pltpu.make_async_remote_copy(
            src_ref=source.at[rows],
            dst_ref=target.at[rows],
            send_sem=send_two.at[which],
            recv_sem=recv_two.at[which],
            device_id=(seq_at, lax.rem(dec_at + 1, owners)),
            device_id_type=MESH,
        )

    start = band_start(band_rows, seq_at, dec_at, owners)
    live = band_rows[seq_at, dec_at]
    fill(0)
    pass_on(0)
    fill(1)
    all_owners(0).wait_recv()
    pass_on(1)
    for copy in loads[3:]:
        copy.wait()
    first_stage(start, got_lat, pick, pairs, spread, taps, w_first, first_out)
    act_first(gain, first_out, conv_a, conv_b)
    for copy in loads[:3]:
        copy.wait()
    second_new(start, gain, w_second, first_out, conv_a, conv_b)
    all_owners(1).wait_recv()
    cache_stage(start, got_act, conv_a, conv_b)

    def leaving(half):
        rows = pl.ds(half * HALF, HALF)
        return pltpu.make_async_copy(staged.at[rows], out.at[rows], load.at[15 + half])

    second_old(
        start,
        live,
        w_second,
        first_out,
        conv_a,
        conv_b,
        staged,
        lambda half: leaving(half).start(),
    )

    for which in range(2):
        for step in range(1, groups):
            to_group(step, which).wait_send()
        all_owners(which).wait_send()
    for half in range(2):
        leaving(half).wait()


def run_block(clip_group, band_rows, new_lat, old_lat, old_act, gain, w_in, w_mid):
    groups = lax.axis_size("seq")
    owners = lax.axis_size("dec")
    per_owner = new_lat.shape[0]
    lat_row, act_row = (PAD_FRAMES, COLS * ZC), (CT * COLS, C)
    bf16 = jnp.bfloat16
    vm = pl.BlockSpec(memory_space=pltpu.VMEM)
    sm = pl.BlockSpec(memory_space=pltpu.SMEM)
    hbm = pl.BlockSpec(memory_space=pl.ANY)
    return pl.pallas_call(
        block,
        out_shape=jax.ShapeDtypeStruct((BAND, ROW, C), bf16),
        in_specs=[sm, sm, hbm, hbm, hbm, vm, hbm, hbm],
        out_specs=hbm,
        scratch_shapes=[
            pltpu.VMEM((BAND, ROW, C), bf16),
            pltpu.VMEM(new_lat.shape, bf16),
            pltpu.VMEM(old_lat.shape, bf16),
            pltpu.VMEM(old_act.shape, bf16),
            pltpu.VMEM((per_owner, COLS * ZC // LANES, groups, PAD_FRAMES, LANES), jnp.float32),
            pltpu.VMEM((per_owner, C // LANES, groups, CT * COLS, LANES), jnp.float32),
            pltpu.VMEM((COLS // TOGETHER, 2 * COLS * ZC, TOGETHER * LANES), bf16),
            pltpu.VMEM((EXT // 2, 2 * PAD_FRAMES, 2 * COLS * ZC), bf16),
            pltpu.VMEM((owners,) + lat_row, bf16),
            pltpu.VMEM((owners,) + act_row, bf16),
            pltpu.VMEM((groups, per_owner) + lat_row, bf16),
            pltpu.VMEM((groups, per_owner) + act_row, bf16),
            pltpu.VMEM((groups, per_owner) + lat_row, bf16),
            pltpu.VMEM((groups, per_owner) + act_row, bf16),
            pltpu.VMEM((owners,) + lat_row, bf16),
            pltpu.VMEM((owners,) + act_row, bf16),
            pltpu.VMEM((768, C), bf16),
            pltpu.VMEM((9 * C, 3 * C), bf16),
            pltpu.VMEM((EXT * PAD_FRAMES * COLS, LANES), jnp.float32),
            pltpu.VMEM((EXT + 1, FRAMES * COLS, LANES), bf16),
            pltpu.VMEM((MID, ROW, C), jnp.float32),
            pltpu.VMEM((SPAN + 1, FRAMES * COLS, 3 * C), bf16),
            pltpu.VMEM((SPAN + 1, FRAMES * COLS, 3 * C), bf16),
            pltpu.SemaphoreType.DMA((2, groups)),
            pltpu.SemaphoreType.DMA((2, groups)),
            pltpu.SemaphoreType.DMA((2,)),
            pltpu.SemaphoreType.DMA((2,)),
            pltpu.SemaphoreType.DMA((17,)),
        ],
        compiler_params=pltpu.CompilerParams(
            collective_id=0, has_side_effects=True, vmem_limit_bytes=56 << 20
        ),
        name="block",
    )(clip_group, band_rows, new_lat, old_lat, old_act, gain, w_in, w_mid)


def shards(latents, cache_lat, cache_act, w_in, w_mid, norm_gain, clip_group, band_rows):
    def by_time(rows):
        return jnp.transpose(rows[0, :, :, 0, :], (1, 0, 2))

    out = run_block(
        clip_group,
        band_rows,
        by_time(latents),
        by_time(cache_lat),
        by_time(cache_act),
        norm_gain,
        w_in.reshape(9, 3 * ZC, C),
        w_mid.reshape(3, 9 * C, C),
    )
    return out.reshape(1, 1, BAND, F, COLS, C)


def solution(mesh):
    placed = P("seq", None, None, "dec", None)
    return jax.shard_map(
        shards,
        mesh=mesh,
        in_specs=(placed, placed, placed, P(), P(), P(), P(), P()),
        out_specs=P("seq", "dec", None, None, None, None),
        check_vma=False,
    )
```

```python
import jax
import jax.numpy as jnp
from jax import lax
from jax.experimental import pallas as pl
from jax.experimental.pallas import tpu as pltpu
from jax.sharding import PartitionSpec as P

F = 4
CT = 2
COLS = 16
ZC = 16
C = 384
FRAMES = F + CT
PAD_FRAMES = 8
ROW = F * COLS
BAND = 24
EXT = BAND + 4
MID = BAND + 2
LANES = 128
TOGETHER = 4
EPSILON = 1e-06
MESH = pl.DeviceIdType.MESH


def band_start(band_rows, group, owner, owners):
    return lax.fori_loop(
        0,
        owners,
        lambda o, total: total + jnp.where(o < owner, band_rows[group, o], 0),
        jnp.int32(0),
    )


def make_pick(pick):
    shape = (2 * COLS * ZC, LANES)
    source = lax.broadcasted_iota(jnp.int32, shape, 0)
    lane = lax.broadcasted_iota(jnp.int32, shape, 1)
    frame = source >= COLS * ZC
    inner = jnp.where(frame, lane - 64, lane)
    here = source & (COLS * ZC - 1)

    inside = (inner >= 0) & (inner < 3 * ZC)

    def some(part, carry):
        for i in range(TOGETHER):
            wanted = here - ZC * (part * TOGETHER + i - 1)
            block = jnp.where(inside & (inner == wanted), 1.0, 0.0).astype(jnp.bfloat16)
            pick[part, :, i * LANES : (i + 1) * LANES] = block
        return carry

    lax.fori_loop(0, COLS // TOGETHER, some, 0)


def first_stage(start, got_lat, pick, pairs, spread, taps, w_first, first_out):
    def gather(i, carry):
        rows = []
        for k in range(2):
            frames = got_lat[(start - 2 + 2 * i + k) & 31].astype(jnp.float32)
            after = pltpu.roll(frames, PAD_FRAMES - 1, 0)
            rows.append(jnp.concatenate([frames, after], axis=1))
        pairs[i] = jnp.concatenate(rows, axis=0).astype(jnp.bfloat16)
        return carry

    lax.fori_loop(0, EXT // 2, gather, 0, unroll=7)
    source = pairs[...].reshape(EXT * PAD_FRAMES, 2 * COLS * ZC)

    def columns(part, carry):
        block = jnp.dot(source, pick[part], preferred_element_type=jnp.float32)
        for i in range(TOGETHER):
            col = part * TOGETHER + i
            rows = pl.ds(col, EXT * PAD_FRAMES, stride=COLS)
            spread[rows, :] = block[:, i * LANES : (i + 1) * LANES]
        return carry

    lax.fori_loop(0, COLS // TOGETHER, columns, 0, unroll=True)
    taps[EXT] = jnp.zeros((FRAMES * COLS, LANES), jnp.bfloat16)

    def narrow(j, carry):
        at = pl.multiple_of(j * PAD_FRAMES * COLS, PAD_FRAMES * COLS)
        taps[j] = spread[pl.ds(at, FRAMES * COLS), :].astype(jnp.bfloat16)
        return carry

    lax.fori_loop(0, EXT, narrow, 0, unroll=7)

    rows = MID // 2
    for part in range(2):
        blocks = []
        for r in range(rows):
            j = part * rows + r + 1
            height = lax.rem(start - 2 + j + 96, 96)
            picks = (
                jnp.where(height == 0, EXT, j - 1),
                j,
                jnp.where(height == 95, EXT, j + 1),
            )
            pieces = []
            for at in picks:
                block = taps[at]
                pieces += [block[:ROW], block[2 * COLS : 2 * COLS + ROW]]
            blocks.append(jnp.concatenate(pieces, axis=1))
        slab = jnp.concatenate(blocks, axis=0)
        total = jnp.dot(slab, w_first[...], preferred_element_type=jnp.float32)
        first_out[part * rows : (part + 1) * rows] = total.reshape(rows, ROW, C)


def shifted(values, position):
    count = values.shape[0]
    before = jnp.where(position == 0, 0.0, pltpu.roll(values, 1, 0))
    after = jnp.where(position == COLS - 1, 0.0, pltpu.roll(values, count - 1, 0))
    return jnp.concatenate([before, values, after], axis=1).astype(jnp.bfloat16)


HALF = BAND // 2
SPAN = HALF + 2


def act_row(row, gain, first_out, position):
    values = first_out[row]
    mean = jnp.mean(values * values, axis=1, keepdims=True)
    half = values * lax.rsqrt(mean + EPSILON) * gain
    return shifted(half + half * jnp.tanh(half), position)


def act_first(gain, first_out, conv_a, conv_b):
    position = lax.broadcasted_iota(jnp.int32, (ROW, C), 0) & (COLS - 1)
    half_gain = 0.5 * gain[...].reshape(1, C)
    zero = jnp.zeros((FRAMES * COLS, 3 * C), jnp.bfloat16)
    conv_a[SPAN] = zero
    conv_b[SPAN] = zero

    def one(i, carry):
        conv_a[i, CT * COLS :] = act_row(i, half_gain, first_out, position)
        return carry

    lax.fori_loop(0, SPAN, one, 0, unroll=7)
    for i in range(2):
        conv_b[i, CT * COLS :] = conv_a[HALF + i, CT * COLS :]


def cache_stage(start, got_act, conv_a, conv_b):
    position = lax.broadcasted_iota(jnp.int32, (CT * COLS, C), 0) & (COLS - 1)

    def one(i, carry):
        for half, conv in enumerate((conv_a, conv_b)):
            at = start - 1 + i + half * HALF
            values = got_act[at & 31].astype(jnp.float32)
            conv[i, : CT * COLS] = shifted(values, position)
        return carry

    lax.fori_loop(0, SPAN, one, 0, unroll=7)


def tap_rows(start, half, row):
    height = lax.rem(start + half * HALF + row, 96)
    return (
        jnp.where(height == 0, SPAN, row),
        row + 1,
        jnp.where(height == 95, SPAN, row + 2),
    )


def slab_of(start, half, frame, frames, conv_in):
    at = frame * COLS
    size = frames * COLS
    blocks = []
    for r in range(HALF):
        picks = tap_rows(start, half, r)
        blocks.append(
            jnp.concatenate([conv_in[row, at : at + size, :] for row in picks], axis=1)
        )
    return jnp.concatenate(blocks, axis=0)


def add_columns(half, frame, frames, low, left, total, first_out):
    size = frames * COLS
    for piece in range(total.shape[1] // LANES):
        column = left + piece * LANES
        tap = low + column // C
        at = (frame - tap) * COLS
        lane = column % C
        for r in range(HALF):
            part = total[r * size : (r + 1) * size, piece * LANES : (piece + 1) * LANES]
            first_out[half * HALF + r + 1, at : at + size, lane : lane + LANES] += part


NEW_FRAMES = ((2, 2, 0, 3), (4, 1, 1, 3), (5, 1, 2, 3))
OLD_FRAMES = ((1, 1, 0, 2), (0, 1, 0, 1))


def products(start, half, groups_of, w_mid, first_out, conv_in, between=None):
    pending = list(between or ())
    tiles = sum(-(-(high - low) * C // 256) for _, _, low, high in groups_of)
    done = 0
    count = len(pending)
    for frame, frames, low, high in groups_of:
        slab = slab_of(start, half, frame, frames, conv_in)
        width = (high - low) * C
        for left in range(0, width, 256):
            right = min(left + 256, width)
            total = jnp.dot(
                slab,
                w_mid[:, low * C + left : low * C + right],
                preferred_element_type=jnp.float32,
            )
            add_columns(half, frame, frames, low, left, total, first_out)
            done += 1
            while pending and (count - len(pending)) < -(-count * done // tiles):
                pending.pop(0)()


def second_new(start, gain, w_mid, first_out, conv_a, conv_b):
    position = lax.broadcasted_iota(jnp.int32, (ROW, C), 0) & (COLS - 1)
    half_gain = 0.5 * gain[...].reshape(1, C)

    def rest(i):
        conv_b[i, CT * COLS :] = act_row(HALF + i, half_gain, first_out, position)

    later = [lambda i=i: rest(i) for i in range(2, SPAN)]
    products(start, 0, NEW_FRAMES, w_mid, first_out, conv_a, later)
    products(start, 1, NEW_FRAMES, w_mid, first_out, conv_b)


def second_old(start, live, w_mid, first_out, conv_a, conv_b, out, leave):
    def emit(r):
        out[r] = jnp.where(r < live, first_out[r + 1], 0.0).astype(jnp.bfloat16)

    def emit_half(half):
        for r in range(half * HALF, (half + 1) * HALF):
            emit(r)
        leave(half)

    products(start, 0, OLD_FRAMES, w_mid, first_out, conv_a)
    products(start, 1, OLD_FRAMES, w_mid, first_out, conv_b, [lambda: emit_half(0)])
    emit_half(1)


def block(
    clip_group,
    band_rows,
    new_lat,
    old_lat,
    old_act,
    gain,
    w_in,
    w_mid,
    out,
    staged,
    raw_new,
    raw_old,
    raw_act,
    rows_lat,
    rows_act,
    pick,
    pairs,
    got_lat,
    got_act,
    clip_lat,
    clip_act,
    stack_lat,
    stack_act,
    slot_lat,
    slot_act,
    w_first,
    w_second,
    spread,
    taps,
    first_out,
    conv_a,
    conv_b,
    send_one,
    recv_one,
    send_two,
    recv_two,
    load,
):
    groups = lax.axis_size("seq")
    owners = lax.axis_size("dec")
    seq_at = lax.axis_index("seq")
    dec_at = lax.axis_index("dec")
    per_owner = new_lat.shape[0]

    raw = [
        pltpu.make_async_copy(new_lat, raw_new, load.at[12]),
        pltpu.make_async_copy(old_lat, raw_old, load.at[13]),
        pltpu.make_async_copy(old_act, raw_act, load.at[14]),
    ]
    loads = [
        pltpu.make_async_copy(
            w_mid.at[tap], w_second.at[:, tap * C : (tap + 1) * C], load.at[9 + tap]
        )
        for tap in range(3)
    ]
    for time_tap in range(3):
        for row_tap in range(3):
            tap = time_tap * 3 + row_tap
            at = row_tap * 256 + time_tap * 64
            loads.append(
                pltpu.make_async_copy(
                    w_in.at[tap], w_first.at[at : at + 3 * ZC, :], load.at[tap]
                )
            )
    for copy in raw + loads[:3]:
        copy.start()

    barrier = pltpu.get_barrier_semaphore()
    for step in range(1, groups):
        pl.semaphore_signal(
            barrier,
            inc=1,
            device_id=(lax.rem(seq_at + step, groups), dec_at),
            device_id_type=MESH,
        )

    def greet(step, carry):
        pl.semaphore_signal(
            barrier,
            inc=1,
            device_id=(seq_at, lax.rem(dec_at + 1 + lax.rem(step + 9, owners - 1), owners)),
            device_id_type=MESH,
        )
        return carry

    lax.fori_loop(1, owners, greet, 0)

    for copy in raw[:2]:
        copy.wait()
    wide = COLS * ZC
    flat_lat = rows_lat.reshape(per_owner, wide // LANES, groups * PAD_FRAMES, LANES)
    flat_act = rows_act.reshape(per_owner, C // LANES, groups * CT * COLS, LANES)
    for t in range(per_owner):
        old = raw_old[t].astype(jnp.float32)
        new = raw_new[t].astype(jnp.float32)
        for frame in range(PAD_FRAMES):
            at = pl.ds(frame, groups, stride=PAD_FRAMES)
            for k in range(wide // LANES):
                lane = frame * wide + k * LANES
                if frame < CT:
                    values = old[:, lane : lane + LANES]
                elif frame < FRAMES:
                    lane -= CT * wide
                    values = new[:, lane : lane + LANES]
                else:
                    values = jnp.zeros((groups, LANES), jnp.float32)
                flat_lat[t, k, at, :] = values

    clips = []
    for group in range(groups):
        clip = jnp.int32(0)
        for i in range(groups):
            clip = clip + jnp.where(clip_group[seq_at, i] == group, i, 0)
        clips.append(jnp.minimum(clip, groups - 1))

    def by_group(rows, target, stack):
        for group in range(groups):
            for t in range(per_owner):
                parts = [rows[t, k, clips[group]] for k in range(rows.shape[1])]
                target[group, t] = jnp.concatenate(parts, axis=1).astype(jnp.bfloat16)
        stack[seq_at] = target[seq_at]

    by_group(rows_lat, clip_lat, stack_lat)
    pl.semaphore_wait(barrier, groups - 1 + owners - 1)

    def to_group(step, which):
        group = lax.rem(seq_at + step, groups)
        source, target = ((clip_lat, stack_lat), (clip_act, stack_act))[which]
        return pltpu.make_async_remote_copy(
            src_ref=source.at[group],
            dst_ref=target.at[seq_at],
            send_sem=send_one.at[which, step],
            recv_sem=recv_one.at[which, step],
            device_id=(group, dec_at),
            device_id_type=MESH,
        )

    for step in (2, 1, 3):
        to_group(step, 0).start()

    raw[2].wait()
    for t in range(per_owner):
        for q in range(CT * COLS):
            at = pl.ds(q, groups, stride=CT * COLS)
            for k in range(C // LANES):
                lane = q * C + k * LANES
                values = raw_act[t, :, lane : lane + LANES].astype(jnp.float32)
                flat_act[t, k, at, :] = values
    by_group(rows_act, clip_act, stack_act)
    for step in range(1, groups):
        to_group(step, 1).start()

    w_first[...] = jnp.zeros_like(w_first)
    for copy in loads[3:]:
        copy.start()
    make_pick(pick)


    def held_row(owner, start):
        first = lax.shift_right_arithmetic(start - 2 - dec_at + owners - 1, 5)
        return jnp.clip(first, 0, groups * per_owner - 1)

    def to_owner(step, which):
        owner = lax.rem(dec_at + 1 + lax.rem(step + 9, owners - 1), owners)
        source, target = ((slot_lat, got_lat), (slot_act, got_act))[which]
        return pltpu.make_async_remote_copy(
            src_ref=source.at[owner],
            dst_ref=target.at[dec_at],
            send_sem=send_two.at[which],
            recv_sem=recv_two.at[which],
            device_id=(seq_at, owner),
            device_id_type=MESH,
        )

    def fill(which):
        stack, slot, got = (
            (stack_lat, slot_lat, got_lat),
            (stack_act, slot_act, got_act),
        )[which]
        for step in range(1, groups):
            to_group(step, which).wait_recv()

        def one(owner, start):
            row = held_row(owner, start)
            slot[owner] = stack[row // per_owner, lax.rem(row, per_owner)]
            return start + band_rows[seq_at, owner]

        lax.fori_loop(0, owners, one, jnp.int32(0), unroll=4)
        got[dec_at] = slot[dec_at]

    def pass_on(which):
        def launch(step, carry):
            to_owner(step, which).start()
            return carry

        lax.fori_loop(1, owners, launch, 0, unroll=True)

    def all_owners(which):
        source, target = ((slot_lat, got_lat), (slot_act, got_act))[which]
        rows = pl.ds(0, owners - 1)
        return pltpu.make_async_remote_copy(
            src_ref=source.at[rows],
            dst_ref=target.at[rows],
            send_sem=send_two.at[which],
            recv_sem=recv_two.at[which],
            device_id=(seq_at, lax.rem(dec_at + 1, owners)),
            device_id_type=MESH,
        )

    start = band_start(band_rows, seq_at, dec_at, owners)
    live = band_rows[seq_at, dec_at]
    fill(0)
    pass_on(0)
    fill(1)
    all_owners(0).wait_recv()
    pass_on(1)
    for copy in loads[3:]:
        copy.wait()
    first_stage(start, got_lat, pick, pairs, spread, taps, w_first, first_out)
    act_first(gain, first_out, conv_a, conv_b)
    for copy in loads[:3]:
        copy.wait()
    second_new(start, gain, w_second, first_out, conv_a, conv_b)
    all_owners(1).wait_recv()
    cache_stage(start, got_act, conv_a, conv_b)

    def leaving(half):
        rows = pl.ds(half * HALF, HALF)
        return pltpu.make_async_copy(staged.at[rows], out.at[rows], load.at[15 + half])

    second_old(
        start,
        live,
        w_second,
        first_out,
        conv_a,
        conv_b,
        staged,
        lambda half: leaving(half).start(),
    )

    for which in range(2):
        for step in range(1, groups):
            to_group(step, which).wait_send()
        all_owners(which).wait_send()
    for half in range(2):
        leaving(half).wait()


def run_block(clip_group, band_rows, new_lat, old_lat, old_act, gain, w_in, w_mid):
    groups = lax.axis_size("seq")
    owners = lax.axis_size("dec")
    per_owner = new_lat.shape[0]
    lat_row, act_row = (PAD_FRAMES, COLS * ZC), (CT * COLS, C)
    bf16 = jnp.bfloat16
    vm = pl.BlockSpec(memory_space=pltpu.VMEM)
    sm = pl.BlockSpec(memory_space=pltpu.SMEM)
    hbm = pl.BlockSpec(memory_space=pl.ANY)
    return pl.pallas_call(
        block,
        out_shape=jax.ShapeDtypeStruct((BAND, ROW, C), bf16),
        in_specs=[sm, sm, hbm, hbm, hbm, vm, hbm, hbm],
        out_specs=hbm,
        scratch_shapes=[
            pltpu.VMEM((BAND, ROW, C), bf16),
            pltpu.VMEM(new_lat.shape, bf16),
            pltpu.VMEM(old_lat.shape, bf16),
            pltpu.VMEM(old_act.shape, bf16),
            pltpu.VMEM((per_owner, COLS * ZC // LANES, groups, PAD_FRAMES, LANES), jnp.float32),
            pltpu.VMEM((per_owner, C // LANES, groups, CT * COLS, LANES), jnp.float32),
            pltpu.VMEM((COLS // TOGETHER, 2 * COLS * ZC, TOGETHER * LANES), bf16),
            pltpu.VMEM((EXT // 2, 2 * PAD_FRAMES, 2 * COLS * ZC), bf16),
            pltpu.VMEM((owners,) + lat_row, bf16),
            pltpu.VMEM((owners,) + act_row, bf16),
            pltpu.VMEM((groups, per_owner) + lat_row, bf16),
            pltpu.VMEM((groups, per_owner) + act_row, bf16),
            pltpu.VMEM((groups, per_owner) + lat_row, bf16),
            pltpu.VMEM((groups, per_owner) + act_row, bf16),
            pltpu.VMEM((owners,) + lat_row, bf16),
            pltpu.VMEM((owners,) + act_row, bf16),
            pltpu.VMEM((768, C), bf16),
            pltpu.VMEM((9 * C, 3 * C), bf16),
            pltpu.VMEM((EXT * PAD_FRAMES * COLS, LANES), jnp.float32),
            pltpu.VMEM((EXT + 1, FRAMES * COLS, LANES), bf16),
            pltpu.VMEM((MID, ROW, C), jnp.float32),
            pltpu.VMEM((SPAN + 1, FRAMES * COLS, 3 * C), bf16),
            pltpu.VMEM((SPAN + 1, FRAMES * COLS, 3 * C), bf16),
            pltpu.SemaphoreType.DMA((2, groups)),
            pltpu.SemaphoreType.DMA((2, groups)),
            pltpu.SemaphoreType.DMA((2,)),
            pltpu.SemaphoreType.DMA((2,)),
            pltpu.SemaphoreType.DMA((17,)),
        ],
        compiler_params=pltpu.CompilerParams(
            collective_id=0, has_side_effects=True, vmem_limit_bytes=56 << 20
        ),
        name="block",
    )(clip_group, band_rows, new_lat, old_lat, old_act, gain, w_in, w_mid)


def shards(latents, cache_lat, cache_act, w_in, w_mid, norm_gain, clip_group, band_rows):
    def by_time(rows):
        return jnp.transpose(rows[0, :, :, 0, :], (1, 0, 2))

    out = run_block(
        clip_group,
        band_rows,
        by_time(latents),
        by_time(cache_lat),
        by_time(cache_act),
        norm_gain,
        w_in.reshape(9, 3 * ZC, C),
        w_mid.reshape(3, 9 * C, C),
    )
    return out.reshape(1, 1, BAND, F, COLS, C)


def solution(mesh):
    placed = P("seq", None, None, "dec", None)
    return jax.shard_map(
        shards,
        mesh=mesh,
        in_specs=(placed, placed, placed, P(), P(), P(), P(), P()),
        out_specs=P("seq", "dec", None, None, None, None),
        check_vma=False,
    )
```

```python
import jax
import jax.numpy as jnp
from jax import lax
from jax.experimental import pallas as pl
from jax.experimental.pallas import tpu as pltpu
from jax.sharding import PartitionSpec as P

F = 4
CT = 2
COLS = 16
ZC = 16
C = 384
FRAMES = F + CT
PAD_FRAMES = 8
ROW = F * COLS
BAND = 24
EXT = BAND + 4
MID = BAND + 2
LANES = 128
TOGETHER = 4
EPSILON = 1e-06
MESH = pl.DeviceIdType.MESH


def band_start(band_rows, group, owner, owners):
    return lax.fori_loop(
        0,
        owners,
        lambda o, total: total + jnp.where(o < owner, band_rows[group, o], 0),
        jnp.int32(0),
    )


def make_pick(pick):
    shape = (2 * COLS * ZC, LANES)
    source = lax.broadcasted_iota(jnp.int32, shape, 0)
    lane = lax.broadcasted_iota(jnp.int32, shape, 1)
    frame = source >= COLS * ZC
    inner = jnp.where(frame, lane - 64, lane)
    here = source & (COLS * ZC - 1)

    inside = (inner >= 0) & (inner < 3 * ZC)

    def some(part, carry):
        for i in range(TOGETHER):
            wanted = here - ZC * (part * TOGETHER + i - 1)
            block = jnp.where(inside & (inner == wanted), 1.0, 0.0).astype(jnp.bfloat16)
            pick[part, :, i * LANES : (i + 1) * LANES] = block
        return carry

    lax.fori_loop(0, COLS // TOGETHER, some, 0)


def first_stage(start, got_lat, pick, pairs, spread, taps, w_first, first_out):
    def gather(i, carry):
        rows = []
        for k in range(2):
            frames = got_lat[(start - 2 + 2 * i + k) & 31].astype(jnp.float32)
            after = pltpu.roll(frames, PAD_FRAMES - 1, 0)
            rows.append(jnp.concatenate([frames, after], axis=1))
        pairs[i] = jnp.concatenate(rows, axis=0).astype(jnp.bfloat16)
        return carry

    lax.fori_loop(0, EXT // 2, gather, 0, unroll=7)
    source = pairs[...].reshape(EXT * PAD_FRAMES, 2 * COLS * ZC)

    def columns(part, carry):
        block = jnp.dot(source, pick[part], preferred_element_type=jnp.float32)
        for i in range(TOGETHER):
            col = part * TOGETHER + i
            rows = pl.ds(col, EXT * PAD_FRAMES, stride=COLS)
            spread[rows, :] = block[:, i * LANES : (i + 1) * LANES]
        return carry

    lax.fori_loop(0, COLS // TOGETHER, columns, 0, unroll=True)
    taps[EXT] = jnp.zeros((FRAMES * COLS, LANES), jnp.bfloat16)

    def narrow(j, carry):
        at = pl.multiple_of(j * PAD_FRAMES * COLS, PAD_FRAMES * COLS)
        taps[j] = spread[pl.ds(at, FRAMES * COLS), :].astype(jnp.bfloat16)
        return carry

    lax.fori_loop(0, EXT, narrow, 0, unroll=True)

    rows = MID // 2
    for part in range(2):
        blocks = []
        for r in range(rows):
            j = part * rows + r + 1
            height = lax.rem(start - 2 + j + 96, 96)
            picks = (
                jnp.where(height == 0, EXT, j - 1),
                j,
                jnp.where(height == 95, EXT, j + 1),
            )
            pieces = []
            for at in picks:
                block = taps[at]
                pieces += [block[:ROW], block[2 * COLS : 2 * COLS + ROW]]
            blocks.append(jnp.concatenate(pieces, axis=1))
        slab = jnp.concatenate(blocks, axis=0)
        total = jnp.dot(slab, w_first[...], preferred_element_type=jnp.float32)
        first_out[part * rows : (part + 1) * rows] = total.reshape(rows, ROW, C)


def shifted(values, position):
    count = values.shape[0]
    before = jnp.where(position == 0, 0.0, pltpu.roll(values, 1, 0))
    after = jnp.where(position == COLS - 1, 0.0, pltpu.roll(values, count - 1, 0))
    return jnp.concatenate([before, values, after], axis=1).astype(jnp.bfloat16)


HALF = BAND // 2
SPAN = HALF + 2


def act_row(row, gain, first_out, position):
    values = first_out[row]
    mean = jnp.mean(values * values, axis=1, keepdims=True)
    half = values * lax.rsqrt(mean + EPSILON) * gain
    return shifted(half + half * jnp.tanh(half), position)


def act_first(gain, first_out, conv_a, conv_b):
    position = lax.broadcasted_iota(jnp.int32, (ROW, C), 0) & (COLS - 1)
    half_gain = 0.5 * gain[...].reshape(1, C)
    zero = jnp.zeros((FRAMES * COLS, 3 * C), jnp.bfloat16)
    conv_a[SPAN] = zero
    conv_b[SPAN] = zero

    def one(i, carry):
        conv_a[i, CT * COLS :] = act_row(i, half_gain, first_out, position)
        return carry

    lax.fori_loop(0, SPAN, one, 0, unroll=True)
    for i in range(2):
        conv_b[i, CT * COLS :] = conv_a[HALF + i, CT * COLS :]


def cache_stage(start, got_act, conv_a, conv_b):
    position = lax.broadcasted_iota(jnp.int32, (CT * COLS, C), 0) & (COLS - 1)

    def one(i, carry):
        for half, conv in enumerate((conv_a, conv_b)):
            at = start - 1 + i + half * HALF
            values = got_act[at & 31].astype(jnp.float32)
            conv[i, : CT * COLS] = shifted(values, position)
        return carry

    lax.fori_loop(0, SPAN, one, 0, unroll=7)


def tap_rows(start, half, row):
    height = lax.rem(start + half * HALF + row, 96)
    return (
        jnp.where(height == 0, SPAN, row),
        row + 1,
        jnp.where(height == 95, SPAN, row + 2),
    )


def slab_of(start, half, frame, frames, conv_in):
    at = frame * COLS
    size = frames * COLS
    blocks = []
    for r in range(HALF):
        picks = tap_rows(start, half, r)
        blocks.append(
            jnp.concatenate([conv_in[row, at : at + size, :] for row in picks], axis=1)
        )
    return jnp.concatenate(blocks, axis=0)


def add_columns(half, frame, frames, low, left, total, first_out):
    size = frames * COLS
    for piece in range(total.shape[1] // LANES):
        column = left + piece * LANES
        tap = low + column // C
        at = (frame - tap) * COLS
        lane = column % C
        for r in range(HALF):
            part = total[r * size : (r + 1) * size, piece * LANES : (piece + 1) * LANES]
            first_out[half * HALF + r + 1, at : at + size, lane : lane + LANES] += part


NEW_FRAMES = ((2, 2, 0, 3), (4, 1, 1, 3), (5, 1, 2, 3))
OLD_FRAMES = ((1, 1, 0, 2), (0, 1, 0, 1))


def products(start, half, groups_of, w_mid, first_out, conv_in, between=None):
    pending = list(between or ())
    tiles = sum(-(-(high - low) * C // 256) for _, _, low, high in groups_of)
    done = 0
    count = len(pending)
    for frame, frames, low, high in groups_of:
        slab = slab_of(start, half, frame, frames, conv_in)
        width = (high - low) * C
        for left in range(0, width, 256):
            right = min(left + 256, width)
            total = jnp.dot(
                slab,
                w_mid[:, low * C + left : low * C + right],
                preferred_element_type=jnp.float32,
            )
            add_columns(half, frame, frames, low, left, total, first_out)
            done += 1
            while pending and (count - len(pending)) < -(-count * done // tiles):
                pending.pop(0)()


def second_new(start, gain, w_mid, first_out, conv_a, conv_b):
    position = lax.broadcasted_iota(jnp.int32, (ROW, C), 0) & (COLS - 1)
    half_gain = 0.5 * gain[...].reshape(1, C)

    def rest(i):
        conv_b[i, CT * COLS :] = act_row(HALF + i, half_gain, first_out, position)

    later = [lambda i=i: rest(i) for i in range(2, SPAN)]
    products(start, 0, NEW_FRAMES, w_mid, first_out, conv_a, later)
    products(start, 1, NEW_FRAMES, w_mid, first_out, conv_b)


def second_old(start, live, w_mid, first_out, conv_a, conv_b, out, leave):
    def emit(r):
        out[r] = jnp.where(r < live, first_out[r + 1], 0.0).astype(jnp.bfloat16)

    def emit_half(half):
        for r in range(half * HALF, (half + 1) * HALF):
            emit(r)
        leave(half)

    products(start, 0, OLD_FRAMES, w_mid, first_out, conv_a)
    products(start, 1, OLD_FRAMES, w_mid, first_out, conv_b, [lambda: emit_half(0)])
    emit_half(1)


def block(
    clip_group,
    band_rows,
    new_lat,
    old_lat,
    old_act,
    gain,
    w_in,
    w_mid,
    out,
    staged,
    raw_new,
    raw_old,
    raw_act,
    rows_lat,
    rows_act,
    pick,
    pairs,
    got_lat,
    got_act,
    clip_lat,
    clip_act,
    stack_lat,
    stack_act,
    slot_lat,
    slot_act,
    w_first,
    w_second,
    spread,
    taps,
    first_out,
    conv_a,
    conv_b,
    send_one,
    recv_one,
    send_two,
    recv_two,
    load,
):
    groups = lax.axis_size("seq")
    owners = lax.axis_size("dec")
    seq_at = lax.axis_index("seq")
    dec_at = lax.axis_index("dec")
    per_owner = new_lat.shape[0]

    raw = [
        pltpu.make_async_copy(new_lat, raw_new, load.at[12]),
        pltpu.make_async_copy(old_lat, raw_old, load.at[13]),
        pltpu.make_async_copy(old_act, raw_act, load.at[14]),
    ]
    loads = [
        pltpu.make_async_copy(
            w_mid.at[tap], w_second.at[:, tap * C : (tap + 1) * C], load.at[9 + tap]
        )
        for tap in range(3)
    ]
    for time_tap in range(3):
        for row_tap in range(3):
            tap = time_tap * 3 + row_tap
            at = row_tap * 256 + time_tap * 64
            loads.append(
                pltpu.make_async_copy(
                    w_in.at[tap], w_first.at[at : at + 3 * ZC, :], load.at[tap]
                )
            )
    for copy in raw + loads[:3]:
        copy.start()

    barrier = pltpu.get_barrier_semaphore()
    for step in range(1, groups):
        pl.semaphore_signal(
            barrier,
            inc=1,
            device_id=(lax.rem(seq_at + step, groups), dec_at),
            device_id_type=MESH,
        )

    def greet(step, carry):
        pl.semaphore_signal(
            barrier,
            inc=1,
            device_id=(seq_at, lax.rem(dec_at + 1 + lax.rem(step + 9, owners - 1), owners)),
            device_id_type=MESH,
        )
        return carry

    lax.fori_loop(1, owners, greet, 0)

    for copy in raw[:2]:
        copy.wait()
    wide = COLS * ZC
    flat_lat = rows_lat.reshape(per_owner, wide // LANES, groups * PAD_FRAMES, LANES)
    flat_act = rows_act.reshape(per_owner, C // LANES, groups * CT * COLS, LANES)
    for t in range(per_owner):
        old = raw_old[t].astype(jnp.float32)
        new = raw_new[t].astype(jnp.float32)
        for frame in range(PAD_FRAMES):
            at = pl.ds(frame, groups, stride=PAD_FRAMES)
            for k in range(wide // LANES):
                lane = frame * wide + k * LANES
                if frame < CT:
                    values = old[:, lane : lane + LANES]
                elif frame < FRAMES:
                    lane -= CT * wide
                    values = new[:, lane : lane + LANES]
                else:
                    values = jnp.zeros((groups, LANES), jnp.float32)
                flat_lat[t, k, at, :] = values

    clips = []
    for group in range(groups):
        clip = jnp.int32(0)
        for i in range(groups):
            clip = clip + jnp.where(clip_group[seq_at, i] == group, i, 0)
        clips.append(jnp.minimum(clip, groups - 1))

    def by_group(rows, target, stack):
        for group in range(groups):
            for t in range(per_owner):
                parts = [rows[t, k, clips[group]] for k in range(rows.shape[1])]
                target[group, t] = jnp.concatenate(parts, axis=1).astype(jnp.bfloat16)
        stack[seq_at] = target[seq_at]

    by_group(rows_lat, clip_lat, stack_lat)
    pl.semaphore_wait(barrier, groups - 1 + owners - 1)

    def to_group(step, which):
        group = lax.rem(seq_at + step, groups)
        source, target = ((clip_lat, stack_lat), (clip_act, stack_act))[which]
        return pltpu.make_async_remote_copy(
            src_ref=source.at[group],
            dst_ref=target.at[seq_at],
            send_sem=send_one.at[which, step],
            recv_sem=recv_one.at[which, step],
            device_id=(group, dec_at),
            device_id_type=MESH,
        )

    for step in (2, 1, 3):
        to_group(step, 0).start()

    raw[2].wait()
    for t in range(per_owner):
        for q in range(CT * COLS):
            at = pl.ds(q, groups, stride=CT * COLS)
            for k in range(C // LANES):
                lane = q * C + k * LANES
                values = raw_act[t, :, lane : lane + LANES].astype(jnp.float32)
                flat_act[t, k, at, :] = values
    by_group(rows_act, clip_act, stack_act)
    for step in range(1, groups):
        to_group(step, 1).start()

    w_first[...] = jnp.zeros_like(w_first)
    for copy in loads[3:]:
        copy.start()
    make_pick(pick)


    def held_row(owner, start):
        first = lax.shift_right_arithmetic(start - 2 - dec_at + owners - 1, 5)
        return jnp.clip(first, 0, groups * per_owner - 1)

    def to_owner(step, which):
        owner = lax.rem(dec_at + 1 + lax.rem(step + 9, owners - 1), owners)
        source, target = ((slot_lat, got_lat), (slot_act, got_act))[which]
        return pltpu.make_async_remote_copy(
            src_ref=source.at[owner],
            dst_ref=target.at[dec_at],
            send_sem=send_two.at[which],
            recv_sem=recv_two.at[which],
            device_id=(seq_at, owner),
            device_id_type=MESH,
        )

    def fill(which):
        stack, slot, got = (
            (stack_lat, slot_lat, got_lat),
            (stack_act, slot_act, got_act),
        )[which]
        for step in range(1, groups):
            to_group(step, which).wait_recv()

        def one(owner, start):
            row = held_row(owner, start)
            slot[owner] = stack[row // per_owner, lax.rem(row, per_owner)]
            return start + band_rows[seq_at, owner]

        lax.fori_loop(0, owners, one, jnp.int32(0), unroll=4)
        got[dec_at] = slot[dec_at]

    def pass_on(which):
        def launch(step, carry):
            to_owner(step, which).start()
            return carry

        lax.fori_loop(1, owners, launch, 0, unroll=True)

    def all_owners(which):
        source, target = ((slot_lat, got_lat), (slot_act, got_act))[which]
        rows = pl.ds(0, owners - 1)
        return pltpu.make_async_remote_copy(
            src_ref=source.at[rows],
            dst_ref=target.at[rows],
            send_sem=send_two.at[which],
            recv_sem=recv_two.at[which],
            device_id=(seq_at, lax.rem(dec_at + 1, owners)),
            device_id_type=MESH,
        )

    start = band_start(band_rows, seq_at, dec_at, owners)
    live = band_rows[seq_at, dec_at]
    fill(0)
    pass_on(0)
    fill(1)
    all_owners(0).wait_recv()
    pass_on(1)
    for copy in loads[3:]:
        copy.wait()
    first_stage(start, got_lat, pick, pairs, spread, taps, w_first, first_out)
    act_first(gain, first_out, conv_a, conv_b)
    for copy in loads[:3]:
        copy.wait()
    second_new(start, gain, w_second, first_out, conv_a, conv_b)
    all_owners(1).wait_recv()
    cache_stage(start, got_act, conv_a, conv_b)

    def leaving(half):
        rows = pl.ds(half * HALF, HALF)
        return pltpu.make_async_copy(staged.at[rows], out.at[rows], load.at[15 + half])

    second_old(
        start,
        live,
        w_second,
        first_out,
        conv_a,
        conv_b,
        staged,
        lambda half: leaving(half).start(),
    )

    for which in range(2):
        for step in range(1, groups):
            to_group(step, which).wait_send()
        all_owners(which).wait_send()
    for half in range(2):
        leaving(half).wait()


def run_block(clip_group, band_rows, new_lat, old_lat, old_act, gain, w_in, w_mid):
    groups = lax.axis_size("seq")
    owners = lax.axis_size("dec")
    per_owner = new_lat.shape[0]
    lat_row, act_row = (PAD_FRAMES, COLS * ZC), (CT * COLS, C)
    bf16 = jnp.bfloat16
    vm = pl.BlockSpec(memory_space=pltpu.VMEM)
    sm = pl.BlockSpec(memory_space=pltpu.SMEM)
    hbm = pl.BlockSpec(memory_space=pl.ANY)
    return pl.pallas_call(
        block,
        out_shape=jax.ShapeDtypeStruct((BAND, ROW, C), bf16),
        in_specs=[sm, sm, hbm, hbm, hbm, vm, hbm, hbm],
        out_specs=hbm,
        scratch_shapes=[
            pltpu.VMEM((BAND, ROW, C), bf16),
            pltpu.VMEM(new_lat.shape, bf16),
            pltpu.VMEM(old_lat.shape, bf16),
            pltpu.VMEM(old_act.shape, bf16),
            pltpu.VMEM((per_owner, COLS * ZC // LANES, groups, PAD_FRAMES, LANES), jnp.float32),
            pltpu.VMEM((per_owner, C // LANES, groups, CT * COLS, LANES), jnp.float32),
            pltpu.VMEM((COLS // TOGETHER, 2 * COLS * ZC, TOGETHER * LANES), bf16),
            pltpu.VMEM((EXT // 2, 2 * PAD_FRAMES, 2 * COLS * ZC), bf16),
            pltpu.VMEM((owners,) + lat_row, bf16),
            pltpu.VMEM((owners,) + act_row, bf16),
            pltpu.VMEM((groups, per_owner) + lat_row, bf16),
            pltpu.VMEM((groups, per_owner) + act_row, bf16),
            pltpu.VMEM((groups, per_owner) + lat_row, bf16),
            pltpu.VMEM((groups, per_owner) + act_row, bf16),
            pltpu.VMEM((owners,) + lat_row, bf16),
            pltpu.VMEM((owners,) + act_row, bf16),
            pltpu.VMEM((768, C), bf16),
            pltpu.VMEM((9 * C, 3 * C), bf16),
            pltpu.VMEM((EXT * PAD_FRAMES * COLS, LANES), jnp.float32),
            pltpu.VMEM((EXT + 1, FRAMES * COLS, LANES), bf16),
            pltpu.VMEM((MID, ROW, C), jnp.float32),
            pltpu.VMEM((SPAN + 1, FRAMES * COLS, 3 * C), bf16),
            pltpu.VMEM((SPAN + 1, FRAMES * COLS, 3 * C), bf16),
            pltpu.SemaphoreType.DMA((2, groups)),
            pltpu.SemaphoreType.DMA((2, groups)),
            pltpu.SemaphoreType.DMA((2,)),
            pltpu.SemaphoreType.DMA((2,)),
            pltpu.SemaphoreType.DMA((17,)),
        ],
        compiler_params=pltpu.CompilerParams(
            collective_id=0, has_side_effects=True, vmem_limit_bytes=56 << 20
        ),
        name="block",
    )(clip_group, band_rows, new_lat, old_lat, old_act, gain, w_in, w_mid)


def shards(latents, cache_lat, cache_act, w_in, w_mid, norm_gain, clip_group, band_rows):
    def by_time(rows):
        return jnp.transpose(rows[0, :, :, 0, :], (1, 0, 2))

    out = run_block(
        clip_group,
        band_rows,
        by_time(latents),
        by_time(cache_lat),
        by_time(cache_act),
        norm_gain,
        w_in.reshape(9, 3 * ZC, C),
        w_mid.reshape(3, 9 * C, C),
    )
    return out.reshape(1, 1, BAND, F, COLS, C)


def solution(mesh):
    placed = P("seq", None, None, "dec", None)
    return jax.shard_map(
        shards,
        mesh=mesh,
        in_specs=(placed, placed, placed, P(), P(), P(), P(), P()),
        out_specs=P("seq", "dec", None, None, None, None),
        check_vma=False,
    )
```
